32 devices in a mesh: tenant: 8 (over z, core), row: 4 (over y, x).
Axes of the slice: x: 2, y: 2, z: 4, core: 2. Of those that a mesh axis runs over, the one named last changes fastest.
Arguments:
- b_factors: float32 [64, 16, 8192], P('tenant', None, 'row'), may hold values from -6 to 6
- a_factors: float32 [64, 16, 8192], P('tenant', None, 'row'), may hold values from -6 to 6
- u_start: float32 [8192, 256], P('row'), may hold values from -0.0625 to 0.0625
- v_start: float32 [8192, 256], P('row'), may hold values from -0.0625 to 0.0625
Outputs:
- u_scaled: float32 [8192, 256], P('row')
- v_scaled: float32 [8192, 256], P('row')
- core_left: float32 [64, 16, 256], P('tenant')
- core_right: float32 [64, 16, 256], P('tenant')
The draws below stay inside these ranges and needn't reach their ends.
All inputs are finite; a program needn't handle non-finite values.
Results may differ from the reference program's by a relative error of at most 0.0003.
Values sent between devices are 32-bit elements; how exact they have to be, the bound alone decides.
A program may use at most 64 MiB of HBM per device.

```python
import math
import jax
import jax.numpy as jnp
from jax import lax

D = 8192
K = 256
R = 16
SWEEPS = 1
NT = 64


def steps_of(stream_key, dims, shards, low, largest):
    def one(axis_at, parts):
        heights = jax.random.uniform(jax.random.fold_in(jax.random.fold_in(stream_key, 6), axis_at), (parts,), jnp.float32, low / len(shards), largest / len(shards))
        return jnp.repeat(jnp.exp(heights), dims[axis_at] // parts).reshape((-1,) + (1,) * (len(dims) - axis_at - 1))

    level = one(*shards[0])
    for cut in shards[1:]:
        level = level * one(*cut)
    return level


def noise(stream_key, shape, scale, limit, cuts=(), kind=jnp.bfloat16):
    drawn = scale * jax.random.normal(stream_key, shape, jnp.float32)
    if cuts:
        drawn = drawn * steps_of(stream_key, shape, cuts, -0.22, 0.18)
    return jnp.clip(drawn, -limit, limit).astype(kind)


def setup_inputs(seed: int = 0) -> dict:
    streams_of = jax.random.split(jax.random.key(seed), 5)
    return {
        "b_factors": noise(streams_of[0], (NT, R, D), 1.0, 6.0, ((0, 8), (2, 4)), jnp.float32),
        "a_factors": noise(streams_of[1], (NT, R, D), 1.0, 6.0, ((0, 8), (2, 4)), jnp.float32),
        "u_start": noise(streams_of[2], (D, K), D ** -0.5, 0.0625, ((0, 4),), jnp.float32),
        "v_start": noise(streams_of[3], (D, K), D ** -0.5, 0.0625, ((0, 4),), jnp.float32),
    }


HIGH = lax.Precision.HIGHEST

def project(factors, basis):
    return jnp.einsum('trd,dk->trk', factors, basis, precision=HIGH)

def orthonormal(matrix):
    gram = jnp.dot(matrix.T, matrix, precision=HIGH)
    lower = jnp.linalg.cholesky(gram)
    return lax.linalg.triangular_solve(lower, matrix, left_side=False, lower=True, transpose_a=True)

def reference(b_factors, a_factors, u_start, v_start):
    left = project(b_factors, u_start)
    right = project(a_factors, v_start)
    basis_u = u_start
    basis_v = v_start
    for sweep in range(SWEEPS):
        weight = jnp.einsum('trk,tsk->trs', right, right, precision=HIGH)
        coeffs = jnp.einsum('trs,tsk->trk', weight, left, precision=HIGH)
        basis_u = orthonormal(jnp.einsum('trd,trk->dk', b_factors, coeffs, precision=HIGH))
        left = project(b_factors, basis_u)
        weight = jnp.einsum('trk,tsk->trs', left, left, precision=HIGH)
        coeffs = jnp.einsum('trs,tsk->trk', weight, right, precision=HIGH)
        basis_v = orthonormal(jnp.einsum('trd,trk->dk', a_factors, coeffs, precision=HIGH))
        right = project(a_factors, basis_v)
    scale = math.sqrt(D)
    return (basis_u * scale, basis_v * scale, left, right)
```

```python
import functools
import math

import jax
import jax.numpy as jnp
from jax import lax
from jax.experimental import pallas as pl
from jax.experimental.pallas import tpu as pltpu
from jax.sharding import PartitionSpec as P

HIGH = lax.Precision.HIGHEST
MESH = pl.DeviceIdType.MESH
VMEM = pl.BlockSpec(memory_space=pltpu.VMEM)
ANY = pl.BlockSpec(memory_space=pl.ANY)
HBM = pl.BlockSpec(memory_space=pltpu.HBM)
BLK = 64
OUT = 4
WIDE = 128
ROOM = 44 << 20
SMALL = 2 << 20
GROUP = 4


def mm(x, y, cx, cy):
    return lax.dot_general(x, y, (((cx,), (cy,)), ((), ())), precision=HIGH, preferred_element_type=jnp.float32)


def split(x):
    top = x.astype(jnp.bfloat16)
    return top, (x - top.astype(jnp.float32)).astype(jnp.bfloat16)


def dot3(x, y, cx, cy):
    (xt, xl), (yt, yl) = x, y
    dot = functools.partial(lax.dot_general, dimension_numbers=(((cx,), (cy,)), ((), ())),
                            preferred_element_type=jnp.float32)
    return dot(xt, yt) + (dot(xt, yl) + dot(xl, yt))


def mm3(x, y, cx, cy):
    return dot3(split(x), split(y), cx, cy)


def remote(src, dst, send, recv, device):
    return pltpu.make_async_remote_copy(
        src_ref=src, dst_ref=dst, send_sem=send, recv_sem=recv, device_id=device, device_id_type=MESH)


def signal(device):
    pl.semaphore_signal(pltpu.get_barrier_semaphore(), inc=1, device_id=device, device_id_type=MESH)


def bits_of(n_row):
    bits = n_row.bit_length() - 1
    assert 1 << bits == n_row
    return bits


def row_partner(bit):
    row = lax.axis_index("row")
    return row + (1 << bit) - 2 * (1 << bit) * (lax.rem(row // (1 << bit), 2))


def row_parts(bits, acc, got, send, recv, base, size):
    half = size // 2

    def copy(step, part):
        bit = (step + part) % bits
        rows = pl.ds(base + part * half, half)
        at = base // size
        return remote(acc.at[step, rows], got.at[step, rows], send.at[at, step, part], recv.at[at, step, part],
                      {"row": row_partner(bit)})

    def begin():
        for part in range(2):
            copy(0, part).start()

    def meet(step):
        for part in range(2):
            rows = pl.ds(base + part * half, half)
            copy(step, part).wait_recv()
            acc[step + 1, rows, :] = acc[step, rows, :] + got[step, rows, :]
            if step + 1 < bits:
                copy(step + 1, part).start()

    def end():
        for step in range(bits):
            for part in range(2):
                copy(step, part).wait_send()

    return begin, meet, end


def factor_block(block):
    n = block.shape[0]
    eye = (lax.broadcasted_iota(jnp.int32, (n, n), 0) == lax.broadcasted_iota(jnp.int32, (n, n), 1)).astype(block.dtype)
    full = jnp.concatenate([block, eye], axis=1)
    groups = [full[8 * g:8 * g + 8, :] for g in range(n // 8)]
    sub = lax.broadcasted_iota(jnp.int32, (8, 2 * n), 0)
    for g in range(n // 8):
        cols = [[jnp.broadcast_to(groups[h][:, 8 * g + c:8 * g + c + 1], (8, 2 * n)) for c in range(8)]
                for h in range(g, n // 8)]
        heads = [[cols[0][c][r:r + 1, :] for c in range(8)] for r in range(8)]
        lines = [groups[g][r:r + 1, :] for r in range(8)]
        invs = []
        for p in range(8):
            inv = 1.0 / heads[p][p]
            invs.append(inv)
            for r in range(p + 1, 8):
                factor = heads[r][p] * inv
                lines[r] = lines[r] - factor * lines[p]
                for c in range(p + 1, 8):
                    heads[r][c] = heads[r][c] - factor * heads[p][c]
        for h in range(g + 1, n // 8):
            col = cols[h - g]
            total = groups[h]
            for p in range(8):
                factor = col[p] * invs[p]
                total = total - factor * lines[p]
                for c in range(p + 1, 8):
                    col[c] = col[c] - factor * heads[p][c]
            groups[h] = total
        group = jnp.broadcast_to(lines[0], (8, 2 * n))
        for r in range(1, 8):
            group = jnp.where(sub == r, lines[r], group)
        groups[g] = group
    full = jnp.concatenate(groups, axis=0)
    diag = jnp.sum(full[:, :n] * eye, axis=1, keepdims=True)
    return full[:, n:] * lax.rsqrt(diag)


def sweep_kernel(bits, chain, rank, scale, b_hbm, a_hbm, u_hbm, v_hbm, fu_hbm, fv_hbm, fleft_ref, fright_ref,
                 f, x, acc, got, own, cs, rs, ctop, clow, mtop, mlow, m, gpart, gmate, gacc, ggot, gfin, lp, lmate, lgot, lcross, lfull, lout,
                 tab, linv_ref, lout_ref, load, row_send, row_recv, own_send, own_recv, own_here, *more):
    c_sems, r_sems = more[:6], more[6:12]
    (gm_send, gm_recv, g_send, g_recv, gf_send, gf_recv, go_send, lm_send, lm_recv, lc_send, lc_recv, rs_send, rs_recv,
     ag_send, ag_recv, lh_send, lh_recv, lo_send, lo_recv, mo_send, m_recv, mp_send, mr_send, mf_send, store) = more[12:]
    tenant, row = lax.axis_index("tenant"), lax.axis_index("row")
    core, place = lax.rem(tenant, 2), tenant // 2
    nt, n_row = 2 * chain, 1 << bits
    low = chain // 2 - 1
    outs = chain // 2 - 1
    side = place // (chain // 2)
    is_mid = jnp.logical_or(place == low, place == low + 1)
    is_out = jnp.logical_not(is_mid)
    is_hub = jnp.logical_and(is_mid, core == 1)
    is_sub = jnp.logical_and(is_mid, core == 0)
    mate = {"tenant": tenant + 1 - 2 * core}
    across = {"tenant": 2 * (2 * low + 1 - place) + core}
    nb = bits + 1
    rows, width = f.shape[1:]
    k = x.shape[2]
    kh = k // 2
    wq = width // 4
    half = nt * rows // 2
    piece = half // n_row
    mine = 2 * side + core

    def outer(j):
        return (1 - side) * (low - 1 - j) + side * (low + 2 + j)

    def out_device(j):
        return {"tenant": 2 * outer(j) + core}

    def neighbour(d):
        to = row
        for bit in range(bits):
            if d >> bit & 1:
                to = to + (1 << bit) - 2 * (1 << bit) * lax.rem(to // (1 << bit), 2)
        return to

    pairs = ((b_hbm, f.at[0]), (u_hbm, x.at[0]), (a_hbm, f.at[1]), (v_hbm, x.at[1]))
    loads = [pltpu.make_async_copy(src, dst, load.at[i]) for i, (src, dst) in enumerate(pairs)]
    for copy in loads:
        copy.start()
    for d in range(1, nt):
        signal({"tenant": lax.rem(tenant + d, nt)})
    for d in range(1, n_row):
        signal({"row": lax.rem(row + d, n_row)})

    @pl.when(is_mid)
    def _():
        for d in range(1, n_row):
            signal({"tenant": 2 * (2 * low + 1 - place) + core, "row": lax.rem(row + d, n_row)})

    def ship(fac, q, lines=None):
        cols = pl.ds(q * wq, wq)
        target = 2 * (low + q // 2) + q % 2
        lines = lines or pl.ds(0, rows)
        sent = remote(f.at[fac, lines, cols], own.at[fac, tenant, lines], own_send.at[fac, q], own_recv.at[fac, tenant],
                      {"tenant": target})
        kept = pltpu.make_async_copy(f.at[fac, :, cols], own.at[fac, tenant], own_here.at[fac])
        return target, sent, kept

    def near(target):
        return target // 2 // (chain // 2) == side

    def far(target):
        return target // 2 // (chain // 2) != side

    def ship_all(fac, some, cores=(0, 1), lines=None):
        for q in [2 * h + c for h in range(2) for c in cores]:
            target, sent, kept = ship(fac, q, lines)

            @pl.when(jnp.logical_and(tenant != target, some(target)))
            def _(sent=sent):
                sent.start()

            if some is not far:
                @pl.when(tenant == target)
                def _(kept=kept):
                    kept.start()

    def ship_end(fac):
        for q in range(4):
            target, sent, kept = ship(fac, q)

            @pl.when(tenant != target)
            def _(sent=sent):
                sent.wait_send()

    def own_wait(fac):
        cols = pl.ds(pl.multiple_of(mine * wq, wq), wq)
        pltpu.make_async_copy(f.at[fac, :, cols], own.at[fac, tenant], own_here.at[fac]).wait()

        def one(i, _):
            @pl.when(i != tenant)
            def _():
                remote(own.at[fac, i], own.at[fac, i], own_send.at[fac, 0], own_recv.at[fac, i], mate).wait_recv()

            return 0

        lax.fori_loop(0, nt, one, 0)

    top, bottom = pl.ds(0, rows // 2), pl.ds(rows // 2, rows - rows // 2)
    tile = 512 if width % 512 == 0 else width
    acc[0] = jnp.zeros_like(acc[0])
    parts = [row_parts(bits, acc, got, row_send, row_recv, fac * rows, rows) for fac in range(2)]
    for fac in range(2):
        loads[2 * fac].wait()
        if fac == 0:
            pl.semaphore_wait(pltpu.get_barrier_semaphore(), nt - 1 + (n_row - 1) * (1 + is_mid.astype(jnp.int32)))

            ship_all(0, near)

            @pl.when(is_mid)
            def _():
                ship_all(0, far)

            @pl.when(is_out)
            def _():
                ship_all(0, far, (1,), top)

        loads[2 * fac + 1].wait()

        def step(i, _, fac=fac):
            cols = pl.ds(pl.multiple_of(i * tile, tile), tile)
            acc[0, pl.ds(fac * rows, rows), :] += mm3(f[fac, :, cols], x[fac, cols, :], 1, 0)
            return 0

        lax.fori_loop(0, width // tile, step, 0)
        parts[fac][0]()
    for at in range(bits):
        for fac in range(2):
            parts[fac][1](at)

    same = lax.broadcasted_iota(jnp.int32, (rows, rows), 0) // rank == lax.broadcasted_iota(
        jnp.int32, (rows, rows), 1) // rank
    rq = rows // n_row
    strip = pl.ds(pl.multiple_of(row * rq, 8), rq)
    below = acc[bits, pl.ds(pl.multiple_of(rows + row * rq, 8), rq), :]
    own_rank = (row * rq + lax.broadcasted_iota(jnp.int32, (rq, rows), 0)) // rank == lax.broadcasted_iota(
        jnp.int32, (rq, rows), 1) // rank
    weight = jnp.where(own_rank, mm(below, acc[bits, rows:, :], 1, 1), 0.0)
    cs[0, place, core, strip, :] = mm(weight, acc[bits, :rows, :], 1, 0)
    rs[place, core, strip, :] = below

    def hand(buf, sems, hop):
        to = low + hop
        part = buf.at[place, core, strip]
        return to, remote(part, part, sems[0].at[hop], sems[1].at[place], {"tenant": 2 * to + core})

    def hand_all(buf, sems):
        for hop in range(2):
            to, sent = hand(buf, sems, hop)

            @pl.when(place != to)
            def _(sent=sent):
                sent.start()

    def spread_copy(buf, sems, d):
        to = neighbour(d)
        part = buf.at[:, core, strip]
        return to, remote(part, part, sems[2].at[d - 1], sems[3].at[row], {"row": to})

    def spread_mate(buf, sems):
        part = buf.at[:, core]
        return remote(part, part, sems[4].at[0], sems[5].at[0], mate)

    def spread_begin(buf, sems):
        def take(i, _):
            @pl.when(i != place)
            def _():
                part = buf.at[i, core, strip]
                remote(part, part, sems[0].at[0], sems[1].at[i], mate).wait_recv()

            return 0

        lax.fori_loop(0, chain, take, 0)
        for d in range(1, n_row):
            spread_copy(buf, sems, d)[1].start()

    def spread_meet(buf, sems):
        for d in range(1, n_row):
            to = spread_copy(buf, sems, d)[0]
            part = buf.at[:, core, pl.ds(pl.multiple_of(to * rq, 8), rq)]
            remote(part, part, sems[2].at[0], sems[3].at[to], mate).wait_recv()
        spread_mate(buf, sems).start()

    def spread_rest(buf, sems):
        part = buf.at[:, 1 - core]
        remote(part, part, sems[4].at[0], sems[5].at[0], mate).wait_recv()

    def spread_end(buf, sems):
        for hop in range(2):
            to, sent = hand(buf, sems, hop)

            @pl.when(place != to)
            def _(sent=sent):
                sent.wait_send()

        @pl.when(is_mid)
        def _():
            for d in range(1, n_row):
                spread_copy(buf, sems, d)[1].wait_send()
            spread_mate(buf, sems).wait_send()

    first = cs.at[0]
    hand_all(first, c_sems)

    hand_all(rs, r_sems)

    @pl.when(is_out)
    def _():
        ship_all(0, far, (1,), bottom)
        ship_all(0, far, (0,))
        ship_all(1, far)

    ship_all(1, near)

    for fac in range(2):
        parts[fac][2]()

    def quarter_out(ph, j):
        return remote(m.at[ph, mine], m.at[ph, mine], mo_send.at[ph, j], m_recv.at[ph, mine], out_device(j))

    def quarter_across(ph, c):
        part = m.at[ph, 2 * side + c]
        return remote(part, part, mp_send.at[ph, c], m_recv.at[ph, 2 * side + c], across)

    def quarter_relay(ph, c, j):
        at = 2 * (1 - side) + c
        return remote(m.at[ph, at], m.at[ph, at], mr_send.at[ph, c, j], m_recv.at[ph, at], out_device(j))

    def quarter_mate(ph, at):
        return remote(m.at[ph, at], m.at[ph, at], mf_send.at[ph, at], m_recv.at[ph, at], mate)

    def quarter_wait(ph, at):
        remote(m.at[ph, at], m.at[ph, at], mp_send.at[ph, 0], m_recv.at[ph, at], mate).wait_recv()

    def cross(ph):
        quarter_across(ph, 0).start()
        quarter_wait(ph, 2 * side + 1)
        quarter_across(ph, 1).start()

    distant = [2 * (1 - side) + c for c in range(2)]

    def relay(ph, c):
        quarter_wait(ph, distant[c])
        quarter_mate(ph, distant[c]).start()
        if c == 0:
            for j in range(outs):
                quarter_relay(ph, c, j).start()

    def relay_hub(ph):
        quarter_wait(ph, distant[1])
        for j in range(outs):
            quarter_relay(ph, 1, j).start()

    def gram_mate(ph):
        return remote(gpart.at[ph], gmate.at[ph], gm_send.at[ph], gm_recv.at[ph], mate)

    def gram_copy(ph, at, part):
        dim = (at + part) % nb
        device = across if dim == bits else {"row": row_partner(dim)}
        return remote(gacc.at[ph, at, part], ggot.at[ph, at, part], g_send.at[ph, at, part], g_recv.at[ph, at, part], device)

    def gram_down(ph):
        return remote(gfin.at[ph], gfin.at[ph], gf_send.at[ph], gf_recv.at[ph], mate)

    def gram_out(ph, j):
        return remote(gfin.at[ph], gfin.at[ph], go_send.at[ph, j], gf_recv.at[ph], out_device(j))

    def gram_meet(ph, at):
        for part in range(3):
            gram_copy(ph, at, part).wait_recv()
            total = gacc[ph, at, part] + ggot[ph, at, part]
            if at + 1 < nb:
                gacc[ph, at + 1, part] = total
                gram_copy(ph, at + 1, part).start()
            else:
                gfin[ph, part] = total

    def left_mate(ph):
        there = pl.ds(pl.multiple_of((1 - core) * half, half), half)
        return remote(lp.at[ph, there], lmate.at[ph], lm_send.at[ph], lm_recv.at[ph], mate)

    def piece_at(at):
        return pl.ds(pl.multiple_of(core * half + at * piece, 8), piece)

    def left_copy(ph, d):
        to = neighbour(d)
        return remote(lp.at[ph, piece_at(to)], lgot.at[ph, row], rs_send.at[ph, d - 1], rs_recv.at[ph, row], {"row": to})

    def left_cross(ph):
        return remote(lp.at[ph, piece_at(row)], lcross.at[ph], lc_send.at[ph], lc_recv.at[ph], across)

    def left_share(ph, d):
        part = lfull.at[ph, piece_at(row)]
        return remote(part, part, ag_send.at[ph, d - 1], ag_recv.at[ph, row], {"row": neighbour(d)})

    def left_half(ph):
        here = pl.ds(pl.multiple_of(core * half, half), half)
        return remote(lfull.at[ph, here], lfull.at[ph, here], lh_send.at[ph], lh_recv.at[ph], mate)

    def left_out(ph, j, c):
        to = 2 * outer(j) + c
        here = pl.ds(pl.multiple_of(to * rows, rows), rows)
        return remote(lfull.at[ph, here], lout.at[ph], lo_send.at[ph, j, c], lo_recv.at[ph], {"tenant": to})

    def left_sum(ph):
        for d in range(1, n_row):
            to = neighbour(d)
            remote(lgot.at[ph, to], lgot.at[ph, to], rs_send.at[ph, 0], rs_recv.at[ph, to], mate).wait_recv()
        total = lp[ph, piece_at(row), :]
        for at in range(n_row):
            total += lgot[ph, at]
        lp[ph, piece_at(row), :] = total
        left_cross(ph).start()

    def left_join(ph):
        left_cross(ph).wait_recv()
        lfull[ph, piece_at(row), :] = lp[ph, piece_at(row), :] + lcross[ph]
        for d in range(1, n_row):
            left_share(ph, d).start()

    lgot[0, row] = jnp.zeros_like(lgot[0, 0])
    lgot[1, row] = jnp.zeros_like(lgot[1, 0])

    def body(ph, _):
        @pl.when(is_mid)
        def _():
            @pl.when(ph == 0)
            def _():
                spread_begin(first, c_sems)
                spread_meet(first, c_sems)
                spread_rest(first, c_sems)

            @pl.when(jnp.logical_and(ph == 1, core == 0))
            def _():
                relay(0, 0)

            own_wait(ph)
            coeffs = cs[ph].reshape(nt * rows, k)
            ctop[...], clow[...] = split(coeffs)

            def columns(j, _):
                cols = pl.ds(pl.multiple_of(j * WIDE, WIDE), WIDE)
                here = pl.ds(pl.multiple_of(j * WIDE, WIDE), WIDE)
                block = own[ph, :, :, cols].reshape(nt * rows, WIDE)
                total = dot3(split(block), (ctop[...], clow[...]), 0, 0)
                m[ph, mine, here, :] = total
                mtop[here, :], mlow[here, :] = split(total)
                return 0

            lax.fori_loop(0, wq // WIDE, columns, 0)
            for j in range(outs):
                quarter_out(ph, j).start()
            quarter_mate(ph, mine).start()
            mq = m.at[ph, mine]
            upper = mm(mq[:, :kh], mq[...], 0, 0)
            grams = (upper[:, :kh], upper[:, kh:], mm(mq[:, kh:], mq[:, kh:], 0, 0))
            for part in range(3):
                gpart[ph, part] = grams[part]

            @pl.when(core == 0)
            def _():
                gram_mate(ph).start()

            @pl.when(core == 1)
            def _():
                gram_mate(ph).wait_recv()
                for part in range(3):
                    gacc[ph, 0, part] = gpart[ph, part] + gmate[ph, part]
                    gram_copy(ph, 0, part).start()

            def lefts(i, _):
                here = pl.ds(pl.multiple_of(i * rows, rows), rows)
                lp[ph, here, :] = dot3(split(own[ph, i]), (mtop[...], mlow[...]), 1, 0)
                return 0

            lax.fori_loop(0, nt, lefts, 0)
            left_mate(ph).start()

            order = sorted(range(1, n_row), key=lambda d: (bin(d).count("1"), d))
            share = -(-len(order) // nb)

            def lefts_ready():
                left_mate(ph).wait_recv()
                here = pl.ds(pl.multiple_of(core * half, half), half)
                lp[ph, here, :] += lmate[ph]

            @pl.when(core == 1)
            def _():
                gram_meet(ph, 0)
                lefts_ready()

                for at in range(nb):
                    if at:
                        gram_meet(ph, at)
                    if at == nb - 1:
                        gram_down(ph).start()
                        for j in range(outs):
                            gram_out(ph, j).start()
                    for d in order[at * share:(at + 1) * share]:
                        left_copy(ph, d).start()

                @pl.when(ph == 1)
                def _():
                    relay_hub(0)

            @pl.when(core == 0)
            def _():
                @pl.when(ph == 1)
                def _():
                    cross(1)

                lefts_ready()

                for d in order:
                    left_copy(ph, d).start()

                @pl.when(ph == 1)
                def _():
                    relay(0, 1)
                    relay(1, 0)

                @pl.when(ph == 0)
                def _():
                    spread_begin(rs, r_sems)
                    ship_all(1, far)

                gram_down(ph).wait_recv()

            @pl.when(jnp.logical_and(ph == 0, core == 1))
            def _():
                spread_begin(rs, r_sems)

            left_sum(ph)

            @pl.when(jnp.logical_and(ph == 0, core == 1))
            def _():
                ship_all(1, far)

        @pl.when(is_out)
        def _():
            gram_down(ph).wait_recv()

            @pl.when(core == 1)
            def _():
                gram_down(ph).start()

        tab[:kh, :kh] = gfin[ph, 0]
        tab[:kh, kh:k] = gfin[ph, 1]
        tab[kh:, kh:k] = gfin[ph, 2]
        tab[:, k:] = (lax.broadcasted_iota(jnp.int32, (k, k), 0) == lax.broadcasted_iota(
            jnp.int32, (k, k), 1)).astype(jnp.float32)
        for at in range(0, k, BLK):
            end = at + BLK
            small = factor_block(tab[at:end, at:end])
            done = mm(small, tab[at:end, at:], 1, 0)
            tab[at:end, at:] = done
            if end < k:
                tab[end:, end:] -= mm(done[:, end - at:k - at], done[:, end - at:], 0, 0)
            if at == BLK:
                @pl.when(jnp.logical_and(is_mid, ph == 0))
                def _():
                    left_join(0)

                @pl.when(jnp.logical_and(is_hub, ph == 1))
                def _():
                    relay_hub(1)
            if at == 0:
                @pl.when(jnp.logical_and(is_mid, ph == 1))
                def _():
                    @pl.when(core == 0)
                    def _():
                        relay(1, 1)

                    left_join(1)
            if at == 2 * BLK:
                @pl.when(is_mid)
                def _():
                    @pl.when(ph == 0)
                    def _():
                        spread_meet(rs, r_sems)

                        @pl.when(core == 0)
                        def _():
                            cross(0)
        linv_ref[ph] = tab[:, k:]

        @pl.when(is_mid)
        def _():
            for d in range(1, n_row):
                part = lfull.at[ph, piece_at(neighbour(d))]
                remote(part, part, ag_send.at[ph, 0], ag_recv.at[ph, neighbour(d)], mate).wait_recv()
            left_half(ph).start()
            left_half(ph).wait_recv()

            @pl.when(ph == 0)
            def _():
                spread_rest(rs, r_sems)

            @pl.when(core == 1)
            def _():
                for j in range(outs):
                    for c in range(2):
                        left_out(ph, j, c).start()

            lout_ref[ph] = lfull[ph, pl.ds(pl.multiple_of(tenant * rows, rows), rows), :]

            @pl.when(ph == 0)
            def _():
                inverse = split(tab[:, k:])

                def some(i, _):
                    group = range(GROUP)
                    ats = [i * GROUP + j for j in group]
                    lefts = [split(dot3(split(lfull[0, pl.ds(pl.multiple_of(at * rows, rows), rows), :]), inverse, 1, 1))
                             for at in ats]
                    weights = [split(jnp.where(same, dot3(left, left, 1, 1), 0.0)) for left in lefts]
                    for j in group:
                        at = ats[j]
                        cs[1, at // 2, at % 2] = dot3(weights[j], split(rs[at // 2, at % 2]), 1, 0)
                    return 0

                lax.fori_loop(0, nt // GROUP, some, 0)

        return 0

    lax.fori_loop(0, 2, body, 0)

    def keep(ph, at):
        here = pl.ds(pl.multiple_of(at * wq, wq), wq)
        return pltpu.make_async_copy(x.at[ph, here], (fu_hbm, fv_hbm)[ph].at[here], store.at[ph, at])

    def quarter_done(ph, at, inverse):
        here = pl.ds(pl.multiple_of(at * wq, wq), wq)
        x[ph, here, :] = dot3(split(m[ph, at]), inverse, 1, 1)

    near_mine, near_mate = mine, 2 * side + 1 - core

    def fetch_near(ph):
        @pl.when(is_out)
        def _():
            quarter_wait(ph, near_mine)
            quarter_mate(ph, near_mine).start()

    def fetch_far(ph):
        @pl.when(is_out)
        def _():
            at = 2 * (1 - side) + core
            quarter_wait(ph, at)
            quarter_mate(ph, at).start()

    def fetch_rest(ph):
        @pl.when(is_out)
        def _():
            quarter_wait(ph, 2 * (1 - side) + 1 - core)

        @pl.when(is_hub)
        def _():
            quarter_wait(ph, distant[0])

    def fetch_mate(ph):
        @pl.when(jnp.logical_or(core == 1, is_out))
        def _():
            quarter_wait(ph, near_mate)

    def fetch_part(ph):
        @pl.when(is_out)
        def _():
            remote(lout.at[ph], lout.at[ph], lo_send.at[ph, 0, 0], lo_recv.at[ph], mate).wait_recv()
            lout_ref[ph] = lout[ph]

        (fleft_ref, fright_ref)[ph][...] = mm3(lout_ref[ph], linv_ref[ph], 1, 1)

    def give(ph, at):
        quarter_done(ph, at, inverses[ph])
        keep(ph, at).start()

    inverses = [split(linv_ref[ph] * scale) for ph in range(2)]
    for ph in range(2):
        fetch_near(ph)
    fetch_far(0)
    give(0, near_mine)
    give(1, near_mine)
    for ph in range(2):
        fetch_mate(ph)
    fetch_rest(0)
    for at in [near_mate] + distant:
        give(0, at)
    give(1, near_mate)
    fetch_far(1)
    give(1, 2 * (1 - side) + core)
    for ph in range(2):
        fetch_part(ph)
    fetch_rest(1)
    give(1, 2 * (1 - side) + 1 - core)
    ship_end(0)
    ship_end(1)
    spread_end(first, c_sems)
    spread_end(rs, r_sems)

    def drain(ph, _):
        quarter_mate(ph, mine).wait_send()

        @pl.when(is_out)
        def _():
            quarter_mate(ph, 2 * (1 - side) + core).wait_send()

        @pl.when(is_mid)
        def _():
            for j in range(outs):
                quarter_out(ph, j).wait_send()
            left_mate(ph).wait_send()
            left_half(ph).wait_send()
            for d in range(1, n_row):
                left_copy(ph, d).wait_send()
                left_share(ph, d).wait_send()
            left_cross(ph).wait_send()

        @pl.when(is_sub)
        def _():
            gram_mate(ph).wait_send()
            for c in range(2):
                quarter_across(ph, c).wait_send()
                quarter_mate(ph, distant[c]).wait_send()
            for j in range(outs):
                quarter_relay(ph, 0, j).wait_send()

        @pl.when(core == 1)
        def _():
            gram_down(ph).wait_send()

        @pl.when(is_hub)
        def _():
            for j in range(outs):
                gram_out(ph, j).wait_send()
                quarter_relay(ph, 1, j).wait_send()
                for c in range(2):
                    left_out(ph, j, c).wait_send()
            for at in range(nb):
                for part in range(3):
                    gram_copy(ph, at, part).wait_send()

        return 0

    lax.fori_loop(0, 2, drain, 0)
    for ph in range(2):
        for at in range(4):
            keep(ph, at).wait()


def sweep(bits, chain, rank, scale, b, a, u, v):
    rows, width = b.shape
    k = u.shape[1]
    kh, wq = k // 2, width // 4
    nt, n_row = 2 * chain, 1 << bits
    outs, nb = max(chain // 2 - 1, 1), bits + 1
    half = nt * rows // 2
    f32, b16 = jnp.float32, jnp.bfloat16
    dma = pltpu.SemaphoreType.DMA
    big, small = jax.ShapeDtypeStruct((width, k), f32), jax.ShapeDtypeStruct((rows, k), f32)
    return pl.pallas_call(
        functools.partial(sweep_kernel, bits, chain, rank, scale),
        out_shape=(big, big, small, small),
        in_specs=[HBM] * 4,
        out_specs=(ANY, ANY, VMEM, VMEM),
        scratch_shapes=[
            pltpu.VMEM((2, rows, width), f32),
            pltpu.VMEM((2, width, k), f32),
            pltpu.VMEM((bits + 1, 2 * rows, k), f32),
            pltpu.VMEM((bits, 2 * rows, k), f32),
            pltpu.VMEM((2, nt, rows, wq), f32),
            pltpu.VMEM((2, chain, 2, rows, k), f32),
            pltpu.VMEM((chain, 2, rows, k), f32),
            pltpu.VMEM((nt * rows, k), b16),
            pltpu.VMEM((nt * rows, k), b16),
            pltpu.VMEM((wq, k), b16),
            pltpu.VMEM((wq, k), b16),
            pltpu.VMEM((2, 4, wq, k), f32),
            pltpu.VMEM((2, 3, kh, kh), f32),
            pltpu.VMEM((2, 3, kh, kh), f32),
            pltpu.VMEM((2, nb, 3, kh, kh), f32),
            pltpu.VMEM((2, nb, 3, kh, kh), f32),
            pltpu.VMEM((2, 3, kh, kh), f32),
            pltpu.VMEM((2, nt * rows, k), f32),
            pltpu.VMEM((2, half, k), f32),
            pltpu.VMEM((2, n_row, half // n_row, k), f32),
            pltpu.VMEM((2, half // n_row, k), f32),
            pltpu.VMEM((2, nt * rows, k), f32),
            pltpu.VMEM((2, rows, k), f32),
            pltpu.VMEM((k, 2 * k), f32),
            pltpu.VMEM((2, k, k), f32),
            pltpu.VMEM((2, rows, k), f32),
            dma((4,)), dma((2, bits, 2)), dma((2, bits, 2)),
            dma((2, 4)), dma((2, nt)), dma((2,)),
            dma((2,)), dma((chain,)), dma((n_row,)), dma((n_row,)), dma((1,)), dma((1,)),
            dma((2,)), dma((chain,)), dma((n_row,)), dma((n_row,)), dma((1,)), dma((1,)),
            dma((2,)), dma((2,)), dma((2, nb, 3)), dma((2, nb, 3)), dma((2,)), dma((2,)), dma((2, outs)),
            dma((2,)), dma((2,)), dma((2,)), dma((2,)), dma((2, n_row)), dma((2, n_row)), dma((2, n_row)), dma((2, n_row)),
            dma((2,)), dma((2,)), dma((2, outs, 2)), dma((2,)),
            dma((2, outs)), dma((2, 4)), dma((2, 2)), dma((2, 2, outs)), dma((2, 4)), dma((2, 4)),
        ],
        compiler_params=pltpu.CompilerParams(collective_id=0, has_side_effects=True, vmem_limit_bytes=ROOM),
    )(b, a, u, v)


def finish_kernel(u_any, v_any, left_in, right_in, fu_hbm, fv_hbm, left_ref, right_ref, store):
    ins, outs = (u_any, v_any), (fu_hbm, fv_hbm)
    size = u_any.shape[0] // OUT
    spots = [(s, i, pl.ds(i * size, size)) for s in range(2) for i in range(OUT)]
    stores = [pltpu.make_async_copy(ins[s].at[at], outs[s].at[at], store.at[s, i]) for s, i, at in spots]
    for copy in stores:
        copy.start()
    left_ref[...] = left_in[...]
    right_ref[...] = right_in[...]
    for copy in stores:
        copy.wait()


def finish(u, v, left, right):
    big, small = jax.ShapeDtypeStruct(u.shape, u.dtype), jax.ShapeDtypeStruct(left.shape, left.dtype)
    return pl.pallas_call(
        finish_kernel,
        out_shape=(big, big, small, small),
        in_specs=[ANY, ANY, VMEM, VMEM],
        out_specs=(HBM, HBM, VMEM, VMEM),
        scratch_shapes=[pltpu.SemaphoreType.DMA((2, OUT))],
        compiler_params=pltpu.CompilerParams(vmem_limit_bytes=SMALL),
    )(u, v, left, right)


def local(mesh_shape, b_factors, a_factors, u_start, v_start):
    nt, rank, width = b_factors.shape
    rows = nt * rank
    k = u_start.shape[1]
    bits = bits_of(mesh_shape["row"])
    chain = mesh_shape["tenant"] // 2
    scale = math.sqrt(width * mesh_shape["row"])
    arrays = (b_factors.reshape(rows, width), a_factors.reshape(rows, width), u_start, v_start)
    swept = sweep(bits, chain, rank, scale, *(pltpu.with_memory_space_constraint(x, pltpu.HBM) for x in arrays))
    u, v, left, right = finish(*swept)
    return u, v, left.reshape(nt, rank, k), right.reshape(nt, rank, k)


def solution(mesh):
    in_specs = (P("tenant", None, "row"), P("tenant", None, "row"), P("row", None), P("row", None))
    out_specs = (P("row", None), P("row", None), P("tenant", None, None), P("tenant", None, None))
    return jax.shard_map(functools.partial(local, dict(mesh.shape)), mesh=mesh, in_specs=in_specs,
                         out_specs=out_specs, check_vma=False)
```

```python
import functools
import math

import jax
import jax.numpy as jnp
from jax import lax
from jax.experimental import pallas as pl
from jax.experimental.pallas import tpu as pltpu
from jax.sharding import PartitionSpec as P

HIGH = lax.Precision.HIGHEST
MESH = pl.DeviceIdType.MESH
VMEM = pl.BlockSpec(memory_space=pltpu.VMEM)
ANY = pl.BlockSpec(memory_space=pl.ANY)
HBM = pl.BlockSpec(memory_space=pltpu.HBM)
BLK = 64
OUT = 4
WIDE = 128
ROOM = 44 << 20
SMALL = 2 << 20
GROUP = 4


def mm(x, y, cx, cy):
    return lax.dot_general(x, y, (((cx,), (cy,)), ((), ())), precision=HIGH, preferred_element_type=jnp.float32)


def split(x):
    top = x.astype(jnp.bfloat16)
    return top, (x - top.astype(jnp.float32)).astype(jnp.bfloat16)


def dot3(x, y, cx, cy):
    (xt, xl), (yt, yl) = x, y
    dot = functools.partial(lax.dot_general, dimension_numbers=(((cx,), (cy,)), ((), ())),
                            preferred_element_type=jnp.float32)
    return dot(xt, yt) + (dot(xt, yl) + dot(xl, yt))


def mm3(x, y, cx, cy):
    return dot3(split(x), split(y), cx, cy)


def remote(src, dst, send, recv, device):
    return pltpu.make_async_remote_copy(
        src_ref=src, dst_ref=dst, send_sem=send, recv_sem=recv, device_id=device, device_id_type=MESH)


def signal(device):
    pl.semaphore_signal(pltpu.get_barrier_semaphore(), inc=1, device_id=device, device_id_type=MESH)


def bits_of(n_row):
    bits = n_row.bit_length() - 1
    assert 1 << bits == n_row
    return bits


def row_partner(bit):
    row = lax.axis_index("row")
    return row + (1 << bit) - 2 * (1 << bit) * (lax.rem(row // (1 << bit), 2))


def row_parts(bits, acc, got, send, recv, base, size):
    half = size // 2

    def copy(step, part):
        bit = (step + part) % bits
        rows = pl.ds(base + part * half, half)
        at = base // size
        return remote(acc.at[step, rows], got.at[step, rows], send.at[at, step, part], recv.at[at, step, part],
                      {"row": row_partner(bit)})

    def begin():
        for part in range(2):
            copy(0, part).start()

    def meet(step):
        for part in range(2):
            rows = pl.ds(base + part * half, half)
            copy(step, part).wait_recv()
            acc[step + 1, rows, :] = acc[step, rows, :] + got[step, rows, :]
            if step + 1 < bits:
                copy(step + 1, part).start()

    def end():
        for step in range(bits):
            for part in range(2):
                copy(step, part).wait_send()

    return begin, meet, end


def factor_block(block):
    n = block.shape[0]
    eye = (lax.broadcasted_iota(jnp.int32, (n, n), 0) == lax.broadcasted_iota(jnp.int32, (n, n), 1)).astype(block.dtype)
    full = jnp.concatenate([block, eye], axis=1)
    groups = [full[8 * g:8 * g + 8, :] for g in range(n // 8)]
    sub = lax.broadcasted_iota(jnp.int32, (8, 2 * n), 0)
    for g in range(n // 8):
        cols = [[jnp.broadcast_to(groups[h][:, 8 * g + c:8 * g + c + 1], (8, 2 * n)) for c in range(8)]
                for h in range(g, n // 8)]
        heads = [[cols[0][c][r:r + 1, :] for c in range(8)] for r in range(8)]
        lines = [groups[g][r:r + 1, :] for r in range(8)]
        invs = []
        for p in range(8):
            inv = 1.0 / heads[p][p]
            invs.append(inv)
            for r in range(p + 1, 8):
                factor = heads[r][p] * inv
                lines[r] = lines[r] - factor * lines[p]
                for c in range(p + 1, 8):
                    heads[r][c] = heads[r][c] - factor * heads[p][c]
        for h in range(g + 1, n // 8):
            col = cols[h - g]
            total = groups[h]
            for p in range(8):
                factor = col[p] * invs[p]
                total = total - factor * lines[p]
                for c in range(p + 1, 8):
                    col[c] = col[c] - factor * heads[p][c]
            groups[h] = total
        group = jnp.broadcast_to(lines[0], (8, 2 * n))
        for r in range(1, 8):
            group = jnp.where(sub == r, lines[r], group)
        groups[g] = group
    full = jnp.concatenate(groups, axis=0)
    diag = jnp.sum(full[:, :n] * eye, axis=1, keepdims=True)
    return full[:, n:] * lax.rsqrt(diag)


def sweep_kernel(bits, chain, rank, scale, b_hbm, a_hbm, u_hbm, v_hbm, fu_hbm, fv_hbm, fleft_ref, fright_ref,
                 f, x, acc, got, own, cs, rs, ctop, clow, mtop, mlow, m, gpart, gmate, gacc, ggot, gfin, lp, lmate, lgot, lcross, lfull, lout,
                 tab, linv_ref, lout_ref, load, row_send, row_recv, own_send, own_recv, own_here, *more):
    c_sems, r_sems = more[:6], more[6:12]
    (gm_send, gm_recv, g_send, g_recv, gf_send, gf_recv, go_send, lm_send, lm_recv, lc_send, lc_recv, rs_send, rs_recv,
     ag_send, ag_recv, lh_send, lh_recv, lo_send, lo_recv, mo_send, m_recv, mp_send, mr_send, mf_send, store) = more[12:]
    tenant, row = lax.axis_index("tenant"), lax.axis_index("row")
    core, place = lax.rem(tenant, 2), tenant // 2
    nt, n_row = 2 * chain, 1 << bits
    low = chain // 2 - 1
    outs = chain // 2 - 1
    side = place // (chain // 2)
    is_mid = jnp.logical_or(place == low, place == low + 1)
    is_out = jnp.logical_not(is_mid)
    is_hub = jnp.logical_and(is_mid, core == 1)
    is_sub = jnp.logical_and(is_mid, core == 0)
    mate = {"tenant": tenant + 1 - 2 * core}
    across = {"tenant": 2 * (2 * low + 1 - place) + core}
    nb = bits + 1
    rows, width = f.shape[1:]
    k = x.shape[2]
    kh = k // 2
    wq = width // 4
    half = nt * rows // 2
    piece = half // n_row
    mine = 2 * side + core

    def outer(j):
        return (1 - side) * (low - 1 - j) + side * (low + 2 + j)

    def out_device(j):
        return {"tenant": 2 * outer(j) + core}

    def neighbour(d):
        to = row
        for bit in range(bits):
            if d >> bit & 1:
                to = to + (1 << bit) - 2 * (1 << bit) * lax.rem(to // (1 << bit), 2)
        return to

    pairs = ((b_hbm, f.at[0]), (u_hbm, x.at[0]), (a_hbm, f.at[1]), (v_hbm, x.at[1]))
    loads = [pltpu.make_async_copy(src, dst, load.at[i]) for i, (src, dst) in enumerate(pairs)]
    for copy in loads:
        copy.start()
    for d in range(1, nt):
        signal({"tenant": lax.rem(tenant + d, nt)})
    for d in range(1, n_row):
        signal({"row": lax.rem(row + d, n_row)})

    @pl.when(is_mid)
    def _():
        for d in range(1, n_row):
            signal({"tenant": 2 * (2 * low + 1 - place) + core, "row": lax.rem(row + d, n_row)})

    def ship(fac, q, lines=None):
        cols = pl.ds(q * wq, wq)
        target = 2 * (low + q // 2) + q % 2
        lines = lines or pl.ds(0, rows)
        sent = remote(f.at[fac, lines, cols], own.at[fac, tenant, lines], own_send.at[fac, q], own_recv.at[fac, tenant],
                      {"tenant": target})
        kept = pltpu.make_async_copy(f.at[fac, :, cols], own.at[fac, tenant], own_here.at[fac])
        return target, sent, kept

    def near(target):
        return target // 2 // (chain // 2) == side

    def far(target):
        return target // 2 // (chain // 2) != side

    def ship_all(fac, some, cores=(0, 1), lines=None):
        for q in [2 * h + c for h in range(2) for c in cores]:
            target, sent, kept = ship(fac, q, lines)

            @pl.when(jnp.logical_and(tenant != target, some(target)))
            def _(sent=sent):
                sent.start()

            if some is not far:
                @pl.when(tenant == target)
                def _(kept=kept):
                    kept.start()

    def ship_end(fac):
        for q in range(4):
            target, sent, kept = ship(fac, q)

            @pl.when(tenant != target)
            def _(sent=sent):
                sent.wait_send()

    def own_wait(fac):
        cols = pl.ds(pl.multiple_of(mine * wq, wq), wq)
        pltpu.make_async_copy(f.at[fac, :, cols], own.at[fac, tenant], own_here.at[fac]).wait()

        def one(i, _):
            @pl.when(i != tenant)
            def _():
                remote(own.at[fac, i], own.at[fac, i], own_send.at[fac, 0], own_recv.at[fac, i], mate).wait_recv()

            return 0

        lax.fori_loop(0, nt, one, 0)

    top, bottom = pl.ds(0, rows // 2), pl.ds(rows // 2, rows - rows // 2)
    tile = 512 if width % 512 == 0 else width
    acc[0] = jnp.zeros_like(acc[0])
    parts = [row_parts(bits, acc, got, row_send, row_recv, fac * rows, rows) for fac in range(2)]
    for fac in range(2):
        loads[2 * fac].wait()
        if fac == 0:
            pl.semaphore_wait(pltpu.get_barrier_semaphore(), nt - 1 + (n_row - 1) * (1 + is_mid.astype(jnp.int32)))

            ship_all(0, near)

            @pl.when(is_mid)
            def _():
                ship_all(0, far)

            @pl.when(is_out)
            def _():
                ship_all(0, far, (1,), top)

        loads[2 * fac + 1].wait()

        def step(i, _, fac=fac):
            cols = pl.ds(pl.multiple_of(i * tile, tile), tile)
            acc[0, pl.ds(fac * rows, rows), :] += mm3(f[fac, :, cols], x[fac, cols, :], 1, 0)
            return 0

        lax.fori_loop(0, width // tile, step, 0)
        parts[fac][0]()
    for at in range(bits):
        for fac in range(2):
            parts[fac][1](at)

    same = lax.broadcasted_iota(jnp.int32, (rows, rows), 0) // rank == lax.broadcasted_iota(
        jnp.int32, (rows, rows), 1) // rank
    rq = rows // n_row
    strip = pl.ds(pl.multiple_of(row * rq, 8), rq)
    below = acc[bits, pl.ds(pl.multiple_of(rows + row * rq, 8), rq), :]
    own_rank = (row * rq + lax.broadcasted_iota(jnp.int32, (rq, rows), 0)) // rank == lax.broadcasted_iota(
        jnp.int32, (rq, rows), 1) // rank
    weight = jnp.where(own_rank, mm(below, acc[bits, rows:, :], 1, 1), 0.0)
    cs[0, place, core, strip, :] = mm(weight, acc[bits, :rows, :], 1, 0)
    rs[place, core, strip, :] = below

    def hand(buf, sems, hop):
        to = low + hop
        part = buf.at[place, core, strip]
        return to, remote(part, part, sems[0].at[hop], sems[1].at[place], {"tenant": 2 * to + core})

    def hand_all(buf, sems):
        for hop in range(2):
            to, sent = hand(buf, sems, hop)

            @pl.when(place != to)
            def _(sent=sent):
                sent.start()

    def spread_copy(buf, sems, d):
        to = neighbour(d)
        part = buf.at[:, core, strip]
        return to, remote(part, part, sems[2].at[d - 1], sems[3].at[row], {"row": to})

    def spread_mate(buf, sems):
        part = buf.at[:, core]
        return remote(part, part, sems[4].at[0], sems[5].at[0], mate)

    def spread_begin(buf, sems):
        def take(i, _):
            @pl.when(i != place)
            def _():
                part = buf.at[i, core, strip]
                remote(part, part, sems[0].at[0], sems[1].at[i], mate).wait_recv()

            return 0

        lax.fori_loop(0, chain, take, 0)
        for d in range(1, n_row):
            spread_copy(buf, sems, d)[1].start()

    def spread_meet(buf, sems):
        for d in range(1, n_row):
            to = spread_copy(buf, sems, d)[0]
            part = buf.at[:, core, pl.ds(pl.multiple_of(to * rq, 8), rq)]
            remote(part, part, sems[2].at[0], sems[3].at[to], mate).wait_recv()
        spread_mate(buf, sems).start()

    def spread_rest(buf, sems):
        part = buf.at[:, 1 - core]
        remote(part, part, sems[4].at[0], sems[5].at[0], mate).wait_recv()

    def spread_end(buf, sems):
        for hop in range(2):
            to, sent = hand(buf, sems, hop)

            @pl.when(place != to)
            def _(sent=sent):
                sent.wait_send()

        @pl.when(is_mid)
        def _():
            for d in range(1, n_row):
                spread_copy(buf, sems, d)[1].wait_send()
            spread_mate(buf, sems).wait_send()

    first = cs.at[0]
    hand_all(first, c_sems)

    hand_all(rs, r_sems)

    @pl.when(is_out)
    def _():
        ship_all(0, far, (1,), bottom)
        ship_all(0, far, (0,))
        ship_all(1, far)

    ship_all(1, near)

    for fac in range(2):
        parts[fac][2]()

    def quarter_out(ph, j):
        return remote(m.at[ph, mine], m.at[ph, mine], mo_send.at[ph, j], m_recv.at[ph, mine], out_device(j))

    def quarter_across(ph, c):
        part = m.at[ph, 2 * side + c]
        return remote(part, part, mp_send.at[ph, c], m_recv.at[ph, 2 * side + c], across)

    def quarter_relay(ph, c, j):
        at = 2 * (1 - side) + c
        return remote(m.at[ph, at], m.at[ph, at], mr_send.at[ph, c, j], m_recv.at[ph, at], out_device(j))

    def quarter_mate(ph, at):
        return remote(m.at[ph, at], m.at[ph, at], mf_send.at[ph, at], m_recv.at[ph, at], mate)

    def quarter_wait(ph, at):
        remote(m.at[ph, at], m.at[ph, at], mp_send.at[ph, 0], m_recv.at[ph, at], mate).wait_recv()

    def cross(ph):
        quarter_across(ph, 0).start()
        quarter_wait(ph, 2 * side + 1)
        quarter_across(ph, 1).start()

    distant = [2 * (1 - side) + c for c in range(2)]

    def relay(ph, c):
        quarter_wait(ph, distant[c])
        quarter_mate(ph, distant[c]).start()
        if c == 0:
            for j in range(outs):
                quarter_relay(ph, c, j).start()

    def relay_hub(ph):
        quarter_wait(ph, distant[1])
        for j in range(outs):
            quarter_relay(ph, 1, j).start()

    def gram_mate(ph):
        return remote(gpart.at[ph], gmate.at[ph], gm_send.at[ph], gm_recv.at[ph], mate)

    def gram_copy(ph, at, part):
        dim = (at + part) % nb
        device = across if dim == bits else {"row": row_partner(dim)}
        return remote(gacc.at[ph, at, part], ggot.at[ph, at, part], g_send.at[ph, at, part], g_recv.at[ph, at, part], device)

    def gram_down(ph):
        return remote(gfin.at[ph], gfin.at[ph], gf_send.at[ph], gf_recv.at[ph], mate)

    def gram_out(ph, j):
        return remote(gfin.at[ph], gfin.at[ph], go_send.at[ph, j], gf_recv.at[ph], out_device(j))

    def gram_meet(ph, at):
        for part in range(3):
            gram_copy(ph, at, part).wait_recv()
            total = gacc[ph, at, part] + ggot[ph, at, part]
            if at + 1 < nb:
                gacc[ph, at + 1, part] = total
                gram_copy(ph, at + 1, part).start()
            else:
                gfin[ph, part] = total

    def left_mate(ph):
        there = pl.ds(pl.multiple_of((1 - core) * half, half), half)
        return remote(lp.at[ph, there], lmate.at[ph], lm_send.at[ph], lm_recv.at[ph], mate)

    def piece_at(at):
        return pl.ds(pl.multiple_of(core * half + at * piece, 8), piece)

    def left_copy(ph, d):
        to = neighbour(d)
        return remote(lp.at[ph, piece_at(to)], lgot.at[ph, row], rs_send.at[ph, d - 1], rs_recv.at[ph, row], {"row": to})

    def left_cross(ph):
        return remote(lp.at[ph, piece_at(row)], lcross.at[ph], lc_send.at[ph], lc_recv.at[ph], across)

    def left_share(ph, d):
        part = lfull.at[ph, piece_at(row)]
        return remote(part, part, ag_send.at[ph, d - 1], ag_recv.at[ph, row], {"row": neighbour(d)})

    def left_half(ph):
        here = pl.ds(pl.multiple_of(core * half, half), half)
        return remote(lfull.at[ph, here], lfull.at[ph, here], lh_send.at[ph], lh_recv.at[ph], mate)

    def left_out(ph, j, c):
        to = 2 * outer(j) + c
        here = pl.ds(pl.multiple_of(to * rows, rows), rows)
        return remote(lfull.at[ph, here], lout.at[ph], lo_send.at[ph, j, c], lo_recv.at[ph], {"tenant": to})

    def left_sum(ph):
        for d in range(1, n_row):
            to = neighbour(d)
            remote(lgot.at[ph, to], lgot.at[ph, to], rs_send.at[ph, 0], rs_recv.at[ph, to], mate).wait_recv()
        total = lp[ph, piece_at(row), :]
        for at in range(n_row):
            total += lgot[ph, at]
        lp[ph, piece_at(row), :] = total
        left_cross(ph).start()

    def left_join(ph):
        left_cross(ph).wait_recv()
        lfull[ph, piece_at(row), :] = lp[ph, piece_at(row), :] + lcross[ph]
        for d in range(1, n_row):
            left_share(ph, d).start()

    lgot[0, row] = jnp.zeros_like(lgot[0, 0])
    lgot[1, row] = jnp.zeros_like(lgot[1, 0])

    def body(ph, _):
        @pl.when(is_mid)
        def _():
            @pl.when(ph == 0)
            def _():
                spread_begin(first, c_sems)
                spread_meet(first, c_sems)
                spread_rest(first, c_sems)

            own_wait(ph)
            coeffs = cs[ph].reshape(nt * rows, k)
            ctop[...], clow[...] = split(coeffs)

            def columns(j, _):
                cols = pl.ds(pl.multiple_of(j * WIDE, WIDE), WIDE)
                here = pl.ds(pl.multiple_of(j * WIDE, WIDE), WIDE)
                block = own[ph, :, :, cols].reshape(nt * rows, WIDE)
                total = dot3(split(block), (ctop[...], clow[...]), 0, 0)
                m[ph, mine, here, :] = total
                mtop[here, :], mlow[here, :] = split(total)
                return 0

            lax.fori_loop(0, wq // WIDE, columns, 0)
            for j in range(outs):
                quarter_out(ph, j).start()
            quarter_mate(ph, mine).start()
            mq = m.at[ph, mine]
            upper = mm(mq[:, :kh], mq[...], 0, 0)
            grams = (upper[:, :kh], upper[:, kh:], mm(mq[:, kh:], mq[:, kh:], 0, 0))
            for part in range(3):
                gpart[ph, part] = grams[part]

            @pl.when(core == 0)
            def _():
                gram_mate(ph).start()

            @pl.when(core == 1)
            def _():
                gram_mate(ph).wait_recv()
                for part in range(3):
                    gacc[ph, 0, part] = gpart[ph, part] + gmate[ph, part]
                    gram_copy(ph, 0, part).start()

            def lefts(i, _):
                here = pl.ds(pl.multiple_of(i * rows, rows), rows)
                lp[ph, here, :] = dot3(split(own[ph, i]), (mtop[...], mlow[...]), 1, 0)
                return 0

            lax.fori_loop(0, nt, lefts, 0)
            left_mate(ph).start()

            order = sorted(range(1, n_row), key=lambda d: (bin(d).count("1"), d))
            share = -(-len(order) // nb)

            def lefts_ready():
                left_mate(ph).wait_recv()
                here = pl.ds(pl.multiple_of(core * half, half), half)
                lp[ph, here, :] += lmate[ph]

            @pl.when(core == 1)
            def _():
                @pl.when(ph == 0)
                def _():
                    lefts_ready()
                    for d in order:
                        left_copy(0, d).start()

                gram_meet(ph, 0)

                @pl.when(ph == 1)
                def _():
                    lefts_ready()

                for at in range(nb):
                    if at == nb - 1:
                        @pl.when(ph == 0)
                        def _():
                            left_sum(0)
                            spread_begin(rs, r_sems)

                    if at:
                        gram_meet(ph, at)
                    if at == nb - 1:
                        gram_down(ph).start()
                        for j in range(outs):
                            gram_out(ph, j).start()

                    @pl.when(ph == 1)
                    def _(at=at):
                        for d in order[at * share:(at + 1) * share]:
                            left_copy(1, d).start()

                @pl.when(ph == 1)
                def _():
                    relay_hub(0)
                    left_sum(1)

            @pl.when(core == 0)
            def _():
                @pl.when(ph == 1)
                def _():
                    cross(1)

                lefts_ready()
                for d in order:
                    left_copy(ph, d).start()

                @pl.when(ph == 1)
                def _():
                    relay(0, 0)
                    relay(0, 1)
                    relay(1, 0)

                @pl.when(ph == 0)
                def _():
                    spread_begin(rs, r_sems)
                    left_sum(0)
                    ship_all(1, far)

                gram_down(ph).wait_recv()

                @pl.when(ph == 1)
                def _():
                    left_sum(1)

            @pl.when(jnp.logical_and(ph == 0, core == 1))
            def _():
                left_join(0)
                ship_all(1, far)

        @pl.when(is_out)
        def _():
            gram_down(ph).wait_recv()

            @pl.when(core == 1)
            def _():
                gram_down(ph).start()

        tab[:kh, :kh] = gfin[ph, 0]
        tab[:kh, kh:k] = gfin[ph, 1]
        tab[kh:, kh:k] = gfin[ph, 2]
        tab[:, k:] = (lax.broadcasted_iota(jnp.int32, (k, k), 0) == lax.broadcasted_iota(
            jnp.int32, (k, k), 1)).astype(jnp.float32)
        for at in range(0, k, BLK):
            end = at + BLK
            small = factor_block(tab[at:end, at:end])
            done = mm(small, tab[at:end, at:], 1, 0)
            tab[at:end, at:] = done
            if end < k:
                tab[end:, end:] -= mm(done[:, end - at:k - at], done[:, end - at:], 0, 0)
            if at == BLK:
                @pl.when(jnp.logical_and(is_hub, ph == 1))
                def _():
                    relay_hub(1)
            if at == 0:
                @pl.when(jnp.logical_and(is_sub, ph == 0))
                def _():
                    left_join(0)

                @pl.when(jnp.logical_and(is_mid, ph == 1))
                def _():
                    @pl.when(core == 0)
                    def _():
                        relay(1, 1)

                    left_join(1)

            if at == 2 * BLK:
                @pl.when(is_mid)
                def _():
                    @pl.when(jnp.logical_and(ph == 0, core == 0))
                    def _():
                        cross(0)
        linv_ref[ph] = tab[:, k:]

        @pl.when(is_mid)
        def _():
            for d in range(1, n_row):
                part = lfull.at[ph, piece_at(neighbour(d))]
                remote(part, part, ag_send.at[ph, 0], ag_recv.at[ph, neighbour(d)], mate).wait_recv()
            left_half(ph).start()

            @pl.when(ph == 0)
            def _():
                spread_meet(rs, r_sems)

            left_half(ph).wait_recv()

            @pl.when(ph == 0)
            def _():
                spread_rest(rs, r_sems)

            @pl.when(core == 1)
            def _():
                for j in range(outs):
                    for c in range(2):
                        left_out(ph, j, c).start()

            lout_ref[ph] = lfull[ph, pl.ds(pl.multiple_of(tenant * rows, rows), rows), :]

            @pl.when(ph == 0)
            def _():
                inverse = split(tab[:, k:])

                def some(i, _):
                    group = range(GROUP)
                    ats = [i * GROUP + j for j in group]
                    lefts = [split(dot3(split(lfull[0, pl.ds(pl.multiple_of(at * rows, rows), rows), :]), inverse, 1, 1))
                             for at in ats]
                    weights = [split(jnp.where(same, dot3(left, left, 1, 1), 0.0)) for left in lefts]
                    for j in group:
                        at = ats[j]
                        cs[1, at // 2, at % 2] = dot3(weights[j], split(rs[at // 2, at % 2]), 1, 0)
                    return 0

                lax.fori_loop(0, nt // GROUP, some, 0)

        return 0

    lax.fori_loop(0, 2, body, 0)

    def keep(ph, at):
        here = pl.ds(pl.multiple_of(at * wq, wq), wq)
        return pltpu.make_async_copy(x.at[ph, here], (fu_hbm, fv_hbm)[ph].at[here], store.at[ph, at])

    def quarter_done(ph, at, inverse):
        here = pl.ds(pl.multiple_of(at * wq, wq), wq)
        x[ph, here, :] = dot3(split(m[ph, at]), inverse, 1, 1)

    near_mine, near_mate = mine, 2 * side + 1 - core

    def fetch_near(ph):
        @pl.when(is_out)
        def _():
            quarter_wait(ph, near_mine)
            quarter_mate(ph, near_mine).start()

    def fetch_far(ph):
        @pl.when(is_out)
        def _():
            at = 2 * (1 - side) + core
            quarter_wait(ph, at)
            quarter_mate(ph, at).start()

    def fetch_rest(ph):
        @pl.when(is_out)
        def _():
            quarter_wait(ph, 2 * (1 - side) + 1 - core)

        @pl.when(is_hub)
        def _():
            quarter_wait(ph, distant[0])

    def fetch_mate(ph):
        @pl.when(jnp.logical_or(core == 1, is_out))
        def _():
            quarter_wait(ph, near_mate)

    def fetch_part(ph):
        @pl.when(is_out)
        def _():
            remote(lout.at[ph], lout.at[ph], lo_send.at[ph, 0, 0], lo_recv.at[ph], mate).wait_recv()
            lout_ref[ph] = lout[ph]

        (fleft_ref, fright_ref)[ph][...] = mm3(lout_ref[ph], linv_ref[ph], 1, 1)

    def give(ph, at):
        quarter_done(ph, at, inverses[ph])
        keep(ph, at).start()

    inverses = [split(linv_ref[ph] * scale) for ph in range(2)]
    for ph in range(2):
        fetch_near(ph)
    fetch_far(0)
    give(0, near_mine)
    give(1, near_mine)
    for ph in range(2):
        fetch_mate(ph)
    fetch_rest(0)
    for at in [near_mate] + distant:
        give(0, at)
    give(1, near_mate)
    fetch_far(1)
    give(1, 2 * (1 - side) + core)
    for ph in range(2):
        fetch_part(ph)
    fetch_rest(1)
    give(1, 2 * (1 - side) + 1 - core)
    ship_end(0)
    ship_end(1)
    spread_end(first, c_sems)
    spread_end(rs, r_sems)

    def drain(ph, _):
        quarter_mate(ph, mine).wait_send()

        @pl.when(is_out)
        def _():
            quarter_mate(ph, 2 * (1 - side) + core).wait_send()

        @pl.when(is_mid)
        def _():
            for j in range(outs):
                quarter_out(ph, j).wait_send()
            left_mate(ph).wait_send()
            left_half(ph).wait_send()
            for d in range(1, n_row):
                left_copy(ph, d).wait_send()
                left_share(ph, d).wait_send()
            left_cross(ph).wait_send()

        @pl.when(is_sub)
        def _():
            gram_mate(ph).wait_send()
            for c in range(2):
                quarter_across(ph, c).wait_send()
                quarter_mate(ph, distant[c]).wait_send()
            for j in range(outs):
                quarter_relay(ph, 0, j).wait_send()

        @pl.when(core == 1)
        def _():
            gram_down(ph).wait_send()

        @pl.when(is_hub)
        def _():
            for j in range(outs):
                gram_out(ph, j).wait_send()
                quarter_relay(ph, 1, j).wait_send()
                for c in range(2):
                    left_out(ph, j, c).wait_send()
            for at in range(nb):
                for part in range(3):
                    gram_copy(ph, at, part).wait_send()

        return 0

    lax.fori_loop(0, 2, drain, 0)
    for ph in range(2):
        for at in range(4):
            keep(ph, at).wait()


def sweep(bits, chain, rank, scale, b, a, u, v):
    rows, width = b.shape
    k = u.shape[1]
    kh, wq = k // 2, width // 4
    nt, n_row = 2 * chain, 1 << bits
    outs, nb = max(chain // 2 - 1, 1), bits + 1
    half = nt * rows // 2
    f32, b16 = jnp.float32, jnp.bfloat16
    dma = pltpu.SemaphoreType.DMA
    big, small = jax.ShapeDtypeStruct((width, k), f32), jax.ShapeDtypeStruct((rows, k), f32)
    return pl.pallas_call(
        functools.partial(sweep_kernel, bits, chain, rank, scale),
        out_shape=(big, big, small, small),
        in_specs=[HBM] * 4,
        out_specs=(ANY, ANY, VMEM, VMEM),
        scratch_shapes=[
            pltpu.VMEM((2, rows, width), f32),
            pltpu.VMEM((2, width, k), f32),
            pltpu.VMEM((bits + 1, 2 * rows, k), f32),
            pltpu.VMEM((bits, 2 * rows, k), f32),
            pltpu.VMEM((2, nt, rows, wq), f32),
            pltpu.VMEM((2, chain, 2, rows, k), f32),
            pltpu.VMEM((chain, 2, rows, k), f32),
            pltpu.VMEM((nt * rows, k), b16),
            pltpu.VMEM((nt * rows, k), b16),
            pltpu.VMEM((wq, k), b16),
            pltpu.VMEM((wq, k), b16),
            pltpu.VMEM((2, 4, wq, k), f32),
            pltpu.VMEM((2, 3, kh, kh), f32),
            pltpu.VMEM((2, 3, kh, kh), f32),
            pltpu.VMEM((2, nb, 3, kh, kh), f32),
            pltpu.VMEM((2, nb, 3, kh, kh), f32),
            pltpu.VMEM((2, 3, kh, kh), f32),
            pltpu.VMEM((2, nt * rows, k), f32),
            pltpu.VMEM((2, half, k), f32),
            pltpu.VMEM((2, n_row, half // n_row, k), f32),
            pltpu.VMEM((2, half // n_row, k), f32),
            pltpu.VMEM((2, nt * rows, k), f32),
            pltpu.VMEM((2, rows, k), f32),
            pltpu.VMEM((k, 2 * k), f32),
            pltpu.VMEM((2, k, k), f32),
            pltpu.VMEM((2, rows, k), f32),
            dma((4,)), dma((2, bits, 2)), dma((2, bits, 2)),
            dma((2, 4)), dma((2, nt)), dma((2,)),
            dma((2,)), dma((chain,)), dma((n_row,)), dma((n_row,)), dma((1,)), dma((1,)),
            dma((2,)), dma((chain,)), dma((n_row,)), dma((n_row,)), dma((1,)), dma((1,)),
            dma((2,)), dma((2,)), dma((2, nb, 3)), dma((2, nb, 3)), dma((2,)), dma((2,)), dma((2, outs)),
            dma((2,)), dma((2,)), dma((2,)), dma((2,)), dma((2, n_row)), dma((2, n_row)), dma((2, n_row)), dma((2, n_row)),
            dma((2,)), dma((2,)), dma((2, outs, 2)), dma((2,)),
            dma((2, outs)), dma((2, 4)), dma((2, 2)), dma((2, 2, outs)), dma((2, 4)), dma((2, 4)),
        ],
        compiler_params=pltpu.CompilerParams(collective_id=0, has_side_effects=True, vmem_limit_bytes=ROOM),
    )(b, a, u, v)


def finish_kernel(u_any, v_any, left_in, right_in, fu_hbm, fv_hbm, left_ref, right_ref, store):
    ins, outs = (u_any, v_any), (fu_hbm, fv_hbm)
    size = u_any.shape[0] // OUT
    spots = [(s, i, pl.ds(i * size, size)) for s in range(2) for i in range(OUT)]
    stores = [pltpu.make_async_copy(ins[s].at[at], outs[s].at[at], store.at[s, i]) for s, i, at in spots]
    for copy in stores:
        copy.start()
    left_ref[...] = left_in[...]
    right_ref[...] = right_in[...]
    for copy in stores:
        copy.wait()


def finish(u, v, left, right):
    big, small = jax.ShapeDtypeStruct(u.shape, u.dtype), jax.ShapeDtypeStruct(left.shape, left.dtype)
    return pl.pallas_call(
        finish_kernel,
        out_shape=(big, big, small, small),
        in_specs=[ANY, ANY, VMEM, VMEM],
        out_specs=(HBM, HBM, VMEM, VMEM),
        scratch_shapes=[pltpu.SemaphoreType.DMA((2, OUT))],
        compiler_params=pltpu.CompilerParams(vmem_limit_bytes=SMALL),
    )(u, v, left, right)


def local(mesh_shape, b_factors, a_factors, u_start, v_start):
    nt, rank, width = b_factors.shape
    rows = nt * rank
    k = u_start.shape[1]
    bits = bits_of(mesh_shape["row"])
    chain = mesh_shape["tenant"] // 2
    scale = math.sqrt(width * mesh_shape["row"])
    arrays = (b_factors.reshape(rows, width), a_factors.reshape(rows, width), u_start, v_start)
    swept = sweep(bits, chain, rank, scale, *(pltpu.with_memory_space_constraint(x, pltpu.HBM) for x in arrays))
    u, v, left, right = finish(*swept)
    return u, v, left.reshape(nt, rank, k), right.reshape(nt, rank, k)


def solution(mesh):
    in_specs = (P("tenant", None, "row"), P("tenant", None, "row"), P("row", None), P("row", None))
    out_specs = (P("row", None), P("row", None), P("tenant", None, None), P("tenant", None, None))
    return jax.shard_map(functools.partial(local, dict(mesh.shape)), mesh=mesh, in_specs=in_specs,
                         out_specs=out_specs, check_vma=False)
```

```python
import functools
import math

import jax
import jax.numpy as jnp
from jax import lax
from jax.experimental import pallas as pl
from jax.experimental.pallas import tpu as pltpu
from jax.sharding import PartitionSpec as P

HIGH = lax.Precision.HIGHEST
MESH = pl.DeviceIdType.MESH
VMEM = pl.BlockSpec(memory_space=pltpu.VMEM)
ANY = pl.BlockSpec(memory_space=pl.ANY)
HBM = pl.BlockSpec(memory_space=pltpu.HBM)
BLK = 64
OUT = 4
WIDE = 256
ROOM = 44 << 20
SMALL = 2 << 20
GROUP = 8


def mm(x, y, cx, cy):
    return lax.dot_general(x, y, (((cx,), (cy,)), ((), ())), precision=HIGH, preferred_element_type=jnp.float32)


def split(x):
    top = x.astype(jnp.bfloat16)
    return top, (x - top.astype(jnp.float32)).astype(jnp.bfloat16)


def dot3(x, y, cx, cy):
    (xt, xl), (yt, yl) = x, y
    dot = functools.partial(lax.dot_general, dimension_numbers=(((cx,), (cy,)), ((), ())),
                            preferred_element_type=jnp.float32)
    return dot(xt, yt) + (dot(xt, yl) + dot(xl, yt))


def mm3(x, y, cx, cy):
    return dot3(split(x), split(y), cx, cy)


def remote(src, dst, send, recv, device):
    return pltpu.make_async_remote_copy(
        src_ref=src, dst_ref=dst, send_sem=send, recv_sem=recv, device_id=device, device_id_type=MESH)


def signal(device):
    pl.semaphore_signal(pltpu.get_barrier_semaphore(), inc=1, device_id=device, device_id_type=MESH)


def bits_of(n_row):
    bits = n_row.bit_length() - 1
    assert 1 << bits == n_row
    return bits


def row_partner(bit):
    row = lax.axis_index("row")
    return row + (1 << bit) - 2 * (1 << bit) * (lax.rem(row // (1 << bit), 2))


def row_parts(bits, acc, got, send, recv, base, size):
    half = size // 2

    def copy(step, part):
        bit = (step + part) % bits
        rows = pl.ds(base + part * half, half)
        at = base // size
        return remote(acc.at[step, rows], got.at[step, rows], send.at[at, step, part], recv.at[at, step, part],
                      {"row": row_partner(bit)})

    def begin():
        for part in range(2):
            copy(0, part).start()

    def meet(step):
        for part in range(2):
            rows = pl.ds(base + part * half, half)
            copy(step, part).wait_recv()
            acc[step + 1, rows, :] = acc[step, rows, :] + got[step, rows, :]
            if step + 1 < bits:
                copy(step + 1, part).start()

    def end():
        for step in range(bits):
            for part in range(2):
                copy(step, part).wait_send()

    return begin, meet, end


def factor_block(block):
    n = block.shape[0]
    eye = (lax.broadcasted_iota(jnp.int32, (n, n), 0) == lax.broadcasted_iota(jnp.int32, (n, n), 1)).astype(block.dtype)
    full = jnp.concatenate([block, eye], axis=1)
    groups = [full[8 * g:8 * g + 8, :] for g in range(n // 8)]
    sub = lax.broadcasted_iota(jnp.int32, (8, 2 * n), 0)
    for g in range(n // 8):
        cols = [[jnp.broadcast_to(groups[h][:, 8 * g + c:8 * g + c + 1], (8, 2 * n)) for c in range(8)]
                for h in range(g, n // 8)]
        heads = [[cols[0][c][r:r + 1, :] for c in range(8)] for r in range(8)]
        lines = [groups[g][r:r + 1, :] for r in range(8)]
        invs = []
        for p in range(8):
            inv = 1.0 / heads[p][p]
            invs.append(inv)
            for r in range(p + 1, 8):
                factor = heads[r][p] * inv
                lines[r] = lines[r] - factor * lines[p]
                for c in range(p + 1, 8):
                    heads[r][c] = heads[r][c] - factor * heads[p][c]
        for h in range(g + 1, n // 8):
            col = cols[h - g]
            total = groups[h]
            for p in range(8):
                factor = col[p] * invs[p]
                total = total - factor * lines[p]
                for c in range(p + 1, 8):
                    col[c] = col[c] - factor * heads[p][c]
            groups[h] = total
        group = jnp.broadcast_to(lines[0], (8, 2 * n))
        for r in range(1, 8):
            group = jnp.where(sub == r, lines[r], group)
        groups[g] = group
    full = jnp.concatenate(groups, axis=0)
    diag = jnp.sum(full[:, :n] * eye, axis=1, keepdims=True)
    return full[:, n:] * lax.rsqrt(diag)


def sweep_kernel(bits, chain, rank, scale, b_hbm, a_hbm, u_hbm, v_hbm, fu_hbm, fv_hbm, fleft_ref, fright_ref,
                 f, x, acc, got, own, cs, rs, ctop, clow, mtop, mlow, m, gpart, gmate, gacc, ggot, gfin, lp, lmate, lgot, lcross, lfull, lout,
                 tab, linv_ref, lout_ref, load, row_send, row_recv, own_send, own_recv, own_here, *more):
    c_sems, r_sems = more[:6], more[6:12]
    (gm_send, gm_recv, g_send, g_recv, gf_send, gf_recv, go_send, lm_send, lm_recv, lc_send, lc_recv, rs_send, rs_recv,
     ag_send, ag_recv, lh_send, lh_recv, lo_send, lo_recv, mo_send, m_recv, mp_send, mr_send, mf_send, store) = more[12:]
    tenant, row = lax.axis_index("tenant"), lax.axis_index("row")
    core, place = lax.rem(tenant, 2), tenant // 2
    nt, n_row = 2 * chain, 1 << bits
    low = chain // 2 - 1
    outs = chain // 2 - 1
    side = place // (chain // 2)
    is_mid = jnp.logical_or(place == low, place == low + 1)
    is_out = jnp.logical_not(is_mid)
    is_hub = jnp.logical_and(is_mid, core == 1)
    is_sub = jnp.logical_and(is_mid, core == 0)
    mate = {"tenant": tenant + 1 - 2 * core}
    across = {"tenant": 2 * (2 * low + 1 - place) + core}
    nb = bits + 1
    rows, width = f.shape[1:]
    k = x.shape[2]
    kh = k // 2
    wq = width // 4
    half = nt * rows // 2
    piece = half // n_row
    mine = 2 * side + core

    def outer(j):
        return (1 - side) * (low - 1 - j) + side * (low + 2 + j)

    def out_device(j):
        return {"tenant": 2 * outer(j) + core}

    def neighbour(d):
        to = row
        for bit in range(bits):
            if d >> bit & 1:
                to = to + (1 << bit) - 2 * (1 << bit) * lax.rem(to // (1 << bit), 2)
        return to

    pairs = ((b_hbm, f.at[0]), (u_hbm, x.at[0]), (a_hbm, f.at[1]), (v_hbm, x.at[1]))
    loads = [pltpu.make_async_copy(src, dst, load.at[i]) for i, (src, dst) in enumerate(pairs)]
    for copy in loads:
        copy.start()
    for d in range(1, nt):
        signal({"tenant": lax.rem(tenant + d, nt)})
    for d in range(1, n_row):
        signal({"row": lax.rem(row + d, n_row)})

    @pl.when(is_mid)
    def _():
        for d in range(1, n_row):
            signal({"tenant": 2 * (2 * low + 1 - place) + core, "row": lax.rem(row + d, n_row)})

    def ship(fac, q, lines=None):
        cols = pl.ds(q * wq, wq)
        target = 2 * (low + q // 2) + q % 2
        lines = lines or pl.ds(0, rows)
        sent = remote(f.at[fac, lines, cols], own.at[fac, tenant, lines], own_send.at[fac, q], own_recv.at[fac, tenant],
                      {"tenant": target})
        kept = pltpu.make_async_copy(f.at[fac, :, cols], own.at[fac, tenant], own_here.at[fac])
        return target, sent, kept

    def near(target):
        return target // 2 // (chain // 2) == side

    def far(target):
        return target // 2 // (chain // 2) != side

    def ship_all(fac, some, cores=(0, 1), lines=None):
        for q in [2 * h + c for h in range(2) for c in cores]:
            target, sent, kept = ship(fac, q, lines)

            @pl.when(jnp.logical_and(tenant != target, some(target)))
            def _(sent=sent):
                sent.start()

            if some is not far:
                @pl.when(tenant == target)
                def _(kept=kept):
                    kept.start()

    def ship_end(fac):
        for q in range(4):
            target, sent, kept = ship(fac, q)

            @pl.when(tenant != target)
            def _(sent=sent):
                sent.wait_send()

    def own_wait(fac):
        cols = pl.ds(pl.multiple_of(mine * wq, wq), wq)
        pltpu.make_async_copy(f.at[fac, :, cols], own.at[fac, tenant], own_here.at[fac]).wait()

        def one(i, _):
            @pl.when(i != tenant)
            def _():
                remote(own.at[fac, i], own.at[fac, i], own_send.at[fac, 0], own_recv.at[fac, i], mate).wait_recv()

            return 0

        lax.fori_loop(0, nt, one, 0)

    top, bottom = pl.ds(0, rows // 2), pl.ds(rows // 2, rows - rows // 2)
    tile = 512 if width % 512 == 0 else width
    acc[0] = jnp.zeros_like(acc[0])
    parts = [row_parts(bits, acc, got, row_send, row_recv, fac * rows, rows) for fac in range(2)]
    for fac in range(2):
        loads[2 * fac].wait()
        if fac == 0:
            pl.semaphore_wait(pltpu.get_barrier_semaphore(), nt - 1 + (n_row - 1) * (1 + is_mid.astype(jnp.int32)))

            ship_all(0, near)

            @pl.when(is_mid)
            def _():
                ship_all(0, far)

            @pl.when(is_out)
            def _():
                ship_all(0, far, (1,), top)

        loads[2 * fac + 1].wait()

        def step(i, _, fac=fac):
            cols = pl.ds(pl.multiple_of(i * tile, tile), tile)
            acc[0, pl.ds(fac * rows, rows), :] += mm3(f[fac, :, cols], x[fac, cols, :], 1, 0)
            return 0

        lax.fori_loop(0, width // tile, step, 0)
        parts[fac][0]()
    for at in range(bits):
        for fac in range(2):
            parts[fac][1](at)

    same = lax.broadcasted_iota(jnp.int32, (rows, rows), 0) // rank == lax.broadcasted_iota(
        jnp.int32, (rows, rows), 1) // rank
    rq = rows // n_row
    strip = pl.ds(pl.multiple_of(row * rq, 8), rq)
    below = acc[bits, pl.ds(pl.multiple_of(rows + row * rq, 8), rq), :]
    own_rank = (row * rq + lax.broadcasted_iota(jnp.int32, (rq, rows), 0)) // rank == lax.broadcasted_iota(
        jnp.int32, (rq, rows), 1) // rank
    weight = jnp.where(own_rank, mm(below, acc[bits, rows:, :], 1, 1), 0.0)
    cs[0, place, core, strip, :] = mm(weight, acc[bits, :rows, :], 1, 0)
    rs[place, core, strip, :] = below

    def hand(buf, sems, hop):
        to = low + hop
        part = buf.at[place, core, strip]
        return to, remote(part, part, sems[0].at[hop], sems[1].at[place], {"tenant": 2 * to + core})

    def hand_all(buf, sems):
        for hop in range(2):
            to, sent = hand(buf, sems, hop)

            @pl.when(place != to)
            def _(sent=sent):
                sent.start()

    def spread_copy(buf, sems, d):
        to = neighbour(d)
        part = buf.at[:, core, strip]
        return to, remote(part, part, sems[2].at[d - 1], sems[3].at[row], {"row": to})

    def spread_mate(buf, sems):
        part = buf.at[:, core]
        return remote(part, part, sems[4].at[0], sems[5].at[0], mate)

    def spread_begin(buf, sems):
        def take(i, _):
            @pl.when(i != place)
            def _():
                part = buf.at[i, core, strip]
                remote(part, part, sems[0].at[0], sems[1].at[i], mate).wait_recv()

            return 0

        lax.fori_loop(0, chain, take, 0)
        for d in range(1, n_row):
            spread_copy(buf, sems, d)[1].start()

    def spread_meet(buf, sems):
        for d in range(1, n_row):
            to = spread_copy(buf, sems, d)[0]
            part = buf.at[:, core, pl.ds(pl.multiple_of(to * rq, 8), rq)]
            remote(part, part, sems[2].at[0], sems[3].at[to], mate).wait_recv()
        spread_mate(buf, sems).start()

    def spread_rest(buf, sems):
        part = buf.at[:, 1 - core]
        remote(part, part, sems[4].at[0], sems[5].at[0], mate).wait_recv()

    def spread_end(buf, sems):
        for hop in range(2):
            to, sent = hand(buf, sems, hop)

            @pl.when(place != to)
            def _(sent=sent):
                sent.wait_send()

        @pl.when(is_mid)
        def _():
            for d in range(1, n_row):
                spread_copy(buf, sems, d)[1].wait_send()
            spread_mate(buf, sems).wait_send()

    first = cs.at[0]
    hand_all(first, c_sems)

    hand_all(rs, r_sems)

    @pl.when(is_out)
    def _():
        ship_all(0, far, (1,), bottom)
        ship_all(0, far, (0,))
        ship_all(1, far)

    ship_all(1, near)

    for fac in range(2):
        parts[fac][2]()

    def quarter_out(ph, j):
        return remote(m.at[ph, mine], m.at[ph, mine], mo_send.at[ph, j], m_recv.at[ph, mine], out_device(j))

    def quarter_across(ph, c):
        part = m.at[ph, 2 * side + c]
        return remote(part, part, mp_send.at[ph, c], m_recv.at[ph, 2 * side + c], across)

    def quarter_relay(ph, c, j):
        at = 2 * (1 - side) + c
        return remote(m.at[ph, at], m.at[ph, at], mr_send.at[ph, c, j], m_recv.at[ph, at], out_device(j))

    def quarter_mate(ph, at):
        return remote(m.at[ph, at], m.at[ph, at], mf_send.at[ph, at], m_recv.at[ph, at], mate)

    def quarter_wait(ph, at):
        remote(m.at[ph, at], m.at[ph, at], mp_send.at[ph, 0], m_recv.at[ph, at], mate).wait_recv()

    def cross(ph):
        quarter_across(ph, 0).start()
        quarter_wait(ph, 2 * side + 1)
        quarter_across(ph, 1).start()

    distant = [2 * (1 - side) + c for c in range(2)]

    def relay(ph, c):
        quarter_wait(ph, distant[c])
        quarter_mate(ph, distant[c]).start()
        if c == 0:
            for j in range(outs):
                quarter_relay(ph, c, j).start()

    def relay_hub(ph):
        quarter_wait(ph, distant[1])
        for j in range(outs):
            quarter_relay(ph, 1, j).start()

    def gram_mate(ph):
        return remote(gpart.at[ph], gmate.at[ph], gm_send.at[ph], gm_recv.at[ph], mate)

    def gram_copy(ph, at, part):
        dim = (at + part) % nb
        device = across if dim == bits else {"row": row_partner(dim)}
        return remote(gacc.at[ph, at, part], ggot.at[ph, at, part], g_send.at[ph, at, part], g_recv.at[ph, at, part], device)

    def gram_down(ph):
        return remote(gfin.at[ph], gfin.at[ph], gf_send.at[ph], gf_recv.at[ph], mate)

    def gram_out(ph, j):
        return remote(gfin.at[ph], gfin.at[ph], go_send.at[ph, j], gf_recv.at[ph], out_device(j))

    def gram_meet(ph, at):
        for part in range(3):
            gram_copy(ph, at, part).wait_recv()
            total = gacc[ph, at, part] + ggot[ph, at, part]
            if at + 1 < nb:
                gacc[ph, at + 1, part] = total
                gram_copy(ph, at + 1, part).start()
            else:
                gfin[ph, part] = total

    def left_mate(ph):
        there = pl.ds(pl.multiple_of((1 - core) * half, half), half)
        return remote(lp.at[ph, there], lmate.at[ph], lm_send.at[ph], lm_recv.at[ph], mate)

    def piece_at(at):
        return pl.ds(pl.multiple_of(core * half + at * piece, 8), piece)

    def left_copy(ph, d):
        to = neighbour(d)
        return remote(lp.at[ph, piece_at(to)], lgot.at[ph, row], rs_send.at[ph, d - 1], rs_recv.at[ph, row], {"row": to})

    def left_cross(ph):
        return remote(lp.at[ph, piece_at(row)], lcross.at[ph], lc_send.at[ph], lc_recv.at[ph], across)

    def left_share(ph, d):
        part = lfull.at[ph, piece_at(row)]
        return remote(part, part, ag_send.at[ph, d - 1], ag_recv.at[ph, row], {"row": neighbour(d)})

    def left_half(ph):
        here = pl.ds(pl.multiple_of(core * half, half), half)
        return remote(lfull.at[ph, here], lfull.at[ph, here], lh_send.at[ph], lh_recv.at[ph], mate)

    def left_out(ph, j, c):
        to = 2 * outer(j) + c
        here = pl.ds(pl.multiple_of(to * rows, rows), rows)
        return remote(lfull.at[ph, here], lout.at[ph], lo_send.at[ph, j, c], lo_recv.at[ph], {"tenant": to})

    def left_sum(ph):
        for d in range(1, n_row):
            to = neighbour(d)
            remote(lgot.at[ph, to], lgot.at[ph, to], rs_send.at[ph, 0], rs_recv.at[ph, to], mate).wait_recv()
        total = lp[ph, piece_at(row), :]
        for at in range(n_row):
            total += lgot[ph, at]
        lp[ph, piece_at(row), :] = total
        left_cross(ph).start()

    def left_join(ph):
        left_cross(ph).wait_recv()
        lfull[ph, piece_at(row), :] = lp[ph, piece_at(row), :] + lcross[ph]
        for d in range(1, n_row):
            left_share(ph, d).start()

    lgot[0, row] = jnp.zeros_like(lgot[0, 0])
    lgot[1, row] = jnp.zeros_like(lgot[1, 0])

    def body(ph, _):
        @pl.when(is_mid)
        def _():
            @pl.when(ph == 0)
            def _():
                spread_begin(first, c_sems)
                spread_meet(first, c_sems)
                spread_rest(first, c_sems)

            own_wait(ph)
            coeffs = cs[ph].reshape(nt * rows, k)
            ctop[...], clow[...] = split(coeffs)

            def columns(j, _):
                cols = pl.ds(pl.multiple_of(j * WIDE, WIDE), WIDE)
                here = pl.ds(pl.multiple_of(j * WIDE, WIDE), WIDE)
                block = own[ph, :, :, cols].reshape(nt * rows, WIDE)
                total = dot3(split(block), (ctop[...], clow[...]), 0, 0)
                m[ph, mine, here, :] = total
                mtop[here, :], mlow[here, :] = split(total)
                return 0

            lax.fori_loop(0, wq // WIDE, columns, 0)
            for j in range(outs):
                quarter_out(ph, j).start()
            quarter_mate(ph, mine).start()
            mq = m.at[ph, mine]
            upper = mm(mq[:, :kh], mq[...], 0, 0)
            grams = (upper[:, :kh], upper[:, kh:], mm(mq[:, kh:], mq[:, kh:], 0, 0))
            for part in range(3):
                gpart[ph, part] = grams[part]

            @pl.when(core == 0)
            def _():
                gram_mate(ph).start()

            @pl.when(core == 1)
            def _():
                gram_mate(ph).wait_recv()
                for part in range(3):
                    gacc[ph, 0, part] = gpart[ph, part] + gmate[ph, part]
                    gram_copy(ph, 0, part).start()

            def lefts(i, _):
                here = pl.ds(pl.multiple_of(i * rows, rows), rows)
                lp[ph, here, :] = dot3(split(own[ph, i]), (mtop[...], mlow[...]), 1, 0)
                return 0

            lax.fori_loop(0, nt, lefts, 0)
            left_mate(ph).start()

            order = sorted(range(1, n_row), key=lambda d: (bin(d).count("1"), d))
            share = -(-len(order) // nb)

            def lefts_ready():
                left_mate(ph).wait_recv()
                here = pl.ds(pl.multiple_of(core * half, half), half)
                lp[ph, here, :] += lmate[ph]

            @pl.when(core == 1)
            def _():
                @pl.when(ph == 0)
                def _():
                    lefts_ready()
                    for d in order:
                        left_copy(0, d).start()

                gram_meet(ph, 0)

                @pl.when(ph == 1)
                def _():
                    lefts_ready()

                for at in range(nb):
                    if at == nb - 1:
                        @pl.when(ph == 0)
                        def _():
                            left_sum(0)
                            spread_begin(rs, r_sems)

                    if at:
                        gram_meet(ph, at)
                    if at == nb - 1:
                        gram_down(ph).start()
                        for j in range(outs):
                            gram_out(ph, j).start()

                    @pl.when(ph == 1)
                    def _(at=at):
                        for d in order[at * share:(at + 1) * share]:
                            left_copy(1, d).start()

                @pl.when(ph == 1)
                def _():
                    relay_hub(0)
                    left_sum(1)

            @pl.when(core == 0)
            def _():
                @pl.when(ph == 1)
                def _():
                    cross(1)

                lefts_ready()
                for d in order:
                    left_copy(ph, d).start()

                @pl.when(ph == 1)
                def _():
                    relay(0, 0)
                    relay(0, 1)
                    left_sum(1)
                    relay(1, 0)

                @pl.when(ph == 0)
                def _():
                    spread_begin(rs, r_sems)
                    left_sum(0)
                    ship_all(1, far)

                gram_down(ph).wait_recv()

            @pl.when(jnp.logical_and(ph == 0, core == 1))
            def _():
                left_join(0)
                ship_all(1, far)

        @pl.when(is_out)
        def _():
            gram_down(ph).wait_recv()

            @pl.when(core == 1)
            def _():
                gram_down(ph).start()

        tab[:kh, :kh] = gfin[ph, 0]
        tab[:kh, kh:k] = gfin[ph, 1]
        tab[kh:, kh:k] = gfin[ph, 2]
        tab[:, k:] = (lax.broadcasted_iota(jnp.int32, (k, k), 0) == lax.broadcasted_iota(
            jnp.int32, (k, k), 1)).astype(jnp.float32)
        for at in range(0, k, BLK):
            end = at + BLK
            small = factor_block(tab[at:end, at:end])
            done = mm(small, tab[at:end, at:], 1, 0)
            tab[at:end, at:] = done
            if end < k:
                tab[end:, end:] -= mm(done[:, end - at:k - at], done[:, end - at:], 0, 0)
            if at == BLK:
                @pl.when(jnp.logical_and(is_hub, ph == 1))
                def _():
                    relay_hub(1)
            if at == 0:
                @pl.when(jnp.logical_and(is_sub, ph == 0))
                def _():
                    left_join(0)

                @pl.when(jnp.logical_and(is_mid, ph == 1))
                def _():
                    left_join(1)

                    @pl.when(core == 0)
                    def _():
                        relay(1, 1)

            if at == 2 * BLK:
                @pl.when(is_mid)
                def _():
                    @pl.when(jnp.logical_and(ph == 0, core == 0))
                    def _():
                        cross(0)
        linv_ref[ph] = tab[:, k:]

        @pl.when(is_mid)
        def _():
            for d in range(1, n_row):
                part = lfull.at[ph, piece_at(neighbour(d))]
                remote(part, part, ag_send.at[ph, 0], ag_recv.at[ph, neighbour(d)], mate).wait_recv()
            left_half(ph).start()

            @pl.when(ph == 0)
            def _():
                spread_meet(rs, r_sems)

            left_half(ph).wait_recv()

            @pl.when(ph == 0)
            def _():
                spread_rest(rs, r_sems)

            @pl.when(core == 1)
            def _():
                for j in range(outs):
                    for c in range(2):
                        left_out(ph, j, c).start()

            lout_ref[ph] = lfull[ph, pl.ds(pl.multiple_of(tenant * rows, rows), rows), :]

            @pl.when(ph == 0)
            def _():
                inverse = split(tab[:, k:])

                def some(i, _):
                    group = range(GROUP)
                    ats = [i * GROUP + j for j in group]
                    lefts = [split(dot3(split(lfull[0, pl.ds(pl.multiple_of(at * rows, rows), rows), :]), inverse, 1, 1))
                             for at in ats]
                    weights = [split(jnp.where(same, dot3(left, left, 1, 1), 0.0)) for left in lefts]
                    for j in group:
                        at = ats[j]
                        cs[1, at // 2, at % 2] = dot3(weights[j], split(rs[at // 2, at % 2]), 1, 0)
                    return 0

                lax.fori_loop(0, nt // GROUP, some, 0)

        return 0

    lax.fori_loop(0, 2, body, 0)

    def keep(ph, at):
        here = pl.ds(pl.multiple_of(at * wq, wq), wq)
        return pltpu.make_async_copy(x.at[ph, here], (fu_hbm, fv_hbm)[ph].at[here], store.at[ph, at])

    def quarter_done(ph, at, inverse):
        here = pl.ds(pl.multiple_of(at * wq, wq), wq)
        x[ph, here, :] = dot3(split(m[ph, at]), inverse, 1, 1)

    near_mine, near_mate = mine, 2 * side + 1 - core

    def fetch_near(ph):
        @pl.when(is_out)
        def _():
            quarter_wait(ph, near_mine)
            quarter_mate(ph, near_mine).start()

    def fetch_far(ph):
        @pl.when(is_out)
        def _():
            at = 2 * (1 - side) + core
            quarter_wait(ph, at)
            quarter_mate(ph, at).start()

    def fetch_rest(ph):
        @pl.when(is_out)
        def _():
            quarter_wait(ph, 2 * (1 - side) + 1 - core)

        @pl.when(is_hub)
        def _():
            quarter_wait(ph, distant[0])

    def fetch_mate(ph):
        @pl.when(jnp.logical_or(core == 1, is_out))
        def _():
            quarter_wait(ph, near_mate)

    def fetch_part(ph):
        @pl.when(is_out)
        def _():
            remote(lout.at[ph], lout.at[ph], lo_send.at[ph, 0, 0], lo_recv.at[ph], mate).wait_recv()
            lout_ref[ph] = lout[ph]

        (fleft_ref, fright_ref)[ph][...] = mm3(lout_ref[ph], linv_ref[ph], 1, 1)

    def give(ph, at):
        quarter_done(ph, at, inverses[ph])
        keep(ph, at).start()

    inverses = [split(linv_ref[ph] * scale) for ph in range(2)]
    for ph in range(2):
        fetch_near(ph)
    fetch_far(0)
    give(0, near_mine)
    give(1, near_mine)
    for ph in range(2):
        fetch_mate(ph)
    fetch_rest(0)
    for at in [near_mate] + distant:
        give(0, at)
    give(1, near_mate)
    fetch_far(1)
    give(1, 2 * (1 - side) + core)
    fetch_part(0)
    fetch_rest(1)
    give(1, 2 * (1 - side) + 1 - core)
    fetch_part(1)
    ship_end(0)
    ship_end(1)
    spread_end(first, c_sems)
    spread_end(rs, r_sems)

    def drain(ph, _):
        quarter_mate(ph, mine).wait_send()

        @pl.when(is_out)
        def _():
            quarter_mate(ph, 2 * (1 - side) + core).wait_send()

        @pl.when(is_mid)
        def _():
            for j in range(outs):
                quarter_out(ph, j).wait_send()
            left_mate(ph).wait_send()
            left_half(ph).wait_send()
            for d in range(1, n_row):
                left_copy(ph, d).wait_send()
                left_share(ph, d).wait_send()
            left_cross(ph).wait_send()

        @pl.when(is_sub)
        def _():
            gram_mate(ph).wait_send()
            for c in range(2):
                quarter_across(ph, c).wait_send()
                quarter_mate(ph, distant[c]).wait_send()
            for j in range(outs):
                quarter_relay(ph, 0, j).wait_send()

        @pl.when(core == 1)
        def _():
            gram_down(ph).wait_send()

        @pl.when(is_hub)
        def _():
            for j in range(outs):
                gram_out(ph, j).wait_send()
                quarter_relay(ph, 1, j).wait_send()
                for c in range(2):
                    left_out(ph, j, c).wait_send()
            for at in range(nb):
                for part in range(3):
                    gram_copy(ph, at, part).wait_send()

        return 0

    lax.fori_loop(0, 2, drain, 0)
    for ph in range(2):
        for at in range(4):
            keep(ph, at).wait()


def sweep(bits, chain, rank, scale, b, a, u, v):
    rows, width = b.shape
    k = u.shape[1]
    kh, wq = k // 2, width // 4
    nt, n_row = 2 * chain, 1 << bits
    outs, nb = max(chain // 2 - 1, 1), bits + 1
    half = nt * rows // 2
    f32, b16 = jnp.float32, jnp.bfloat16
    dma = pltpu.SemaphoreType.DMA
    big, small = jax.ShapeDtypeStruct((width, k), f32), jax.ShapeDtypeStruct((rows, k), f32)
    return pl.pallas_call(
        functools.partial(sweep_kernel, bits, chain, rank, scale),
        out_shape=(big, big, small, small),
        in_specs=[HBM] * 4,
        out_specs=(ANY, ANY, VMEM, VMEM),
        scratch_shapes=[
            pltpu.VMEM((2, rows, width), f32),
            pltpu.VMEM((2, width, k), f32),
            pltpu.VMEM((bits + 1, 2 * rows, k), f32),
            pltpu.VMEM((bits, 2 * rows, k), f32),
            pltpu.VMEM((2, nt, rows, wq), f32),
            pltpu.VMEM((2, chain, 2, rows, k), f32),
            pltpu.VMEM((chain, 2, rows, k), f32),
            pltpu.VMEM((nt * rows, k), b16),
            pltpu.VMEM((nt * rows, k), b16),
            pltpu.VMEM((wq, k), b16),
            pltpu.VMEM((wq, k), b16),
            pltpu.VMEM((2, 4, wq, k), f32),
            pltpu.VMEM((2, 3, kh, kh), f32),
            pltpu.VMEM((2, 3, kh, kh), f32),
            pltpu.VMEM((2, nb, 3, kh, kh), f32),
            pltpu.VMEM((2, nb, 3, kh, kh), f32),
            pltpu.VMEM((2, 3, kh, kh), f32),
            pltpu.VMEM((2, nt * rows, k), f32),
            pltpu.VMEM((2, half, k), f32),
            pltpu.VMEM((2, n_row, half // n_row, k), f32),
            pltpu.VMEM((2, half // n_row, k), f32),
            pltpu.VMEM((2, nt * rows, k), f32),
            pltpu.VMEM((2, rows, k), f32),
            pltpu.VMEM((k, 2 * k), f32),
            pltpu.VMEM((2, k, k), f32),
            pltpu.VMEM((2, rows, k), f32),
            dma((4,)), dma((2, bits, 2)), dma((2, bits, 2)),
            dma((2, 4)), dma((2, nt)), dma((2,)),
            dma((2,)), dma((chain,)), dma((n_row,)), dma((n_row,)), dma((1,)), dma((1,)),
            dma((2,)), dma((chain,)), dma((n_row,)), dma((n_row,)), dma((1,)), dma((1,)),
            dma((2,)), dma((2,)), dma((2, nb, 3)), dma((2, nb, 3)), dma((2,)), dma((2,)), dma((2, outs)),
            dma((2,)), dma((2,)), dma((2,)), dma((2,)), dma((2, n_row)), dma((2, n_row)), dma((2, n_row)), dma((2, n_row)),
            dma((2,)), dma((2,)), dma((2, outs, 2)), dma((2,)),
            dma((2, outs)), dma((2, 4)), dma((2, 2)), dma((2, 2, outs)), dma((2, 4)), dma((2, 4)),
        ],
        compiler_params=pltpu.CompilerParams(collective_id=0, has_side_effects=True, vmem_limit_bytes=ROOM),
    )(b, a, u, v)


def finish_kernel(u_any, v_any, left_in, right_in, fu_hbm, fv_hbm, left_ref, right_ref, store):
    ins, outs = (u_any, v_any), (fu_hbm, fv_hbm)
    size = u_any.shape[0] // OUT
    spots = [(s, i, pl.ds(i * size, size)) for s in range(2) for i in range(OUT)]
    stores = [pltpu.make_async_copy(ins[s].at[at], outs[s].at[at], store.at[s, i]) for s, i, at in spots]
    for copy in stores:
        copy.start()
    left_ref[...] = left_in[...]
    right_ref[...] = right_in[...]
    for copy in stores:
        copy.wait()


def finish(u, v, left, right):
    big, small = jax.ShapeDtypeStruct(u.shape, u.dtype), jax.ShapeDtypeStruct(left.shape, left.dtype)
    return pl.pallas_call(
        finish_kernel,
        out_shape=(big, big, small, small),
        in_specs=[ANY, ANY, VMEM, VMEM],
        out_specs=(HBM, HBM, VMEM, VMEM),
        scratch_shapes=[pltpu.SemaphoreType.DMA((2, OUT))],
        compiler_params=pltpu.CompilerParams(vmem_limit_bytes=SMALL),
    )(u, v, left, right)


def local(mesh_shape, b_factors, a_factors, u_start, v_start):
    nt, rank, width = b_factors.shape
    rows = nt * rank
    k = u_start.shape[1]
    bits = bits_of(mesh_shape["row"])
    chain = mesh_shape["tenant"] // 2
    scale = math.sqrt(width * mesh_shape["row"])
    arrays = (b_factors.reshape(rows, width), a_factors.reshape(rows, width), u_start, v_start)
    swept = sweep(bits, chain, rank, scale, *(pltpu.with_memory_space_constraint(x, pltpu.HBM) for x in arrays))
    u, v, left, right = finish(*swept)
    return u, v, left.reshape(nt, rank, k), right.reshape(nt, rank, k)


def solution(mesh):
    in_specs = (P("tenant", None, "row"), P("tenant", None, "row"), P("row", None), P("row", None))
    out_specs = (P("row", None), P("row", None), P("tenant", None, None), P("tenant", None, None))
    return jax.shard_map(functools.partial(local, dict(mesh.shape)), mesh=mesh, in_specs=in_specs,
                         out_specs=out_specs, check_vma=False)
```

```python
import functools
import math

import jax
import jax.numpy as jnp
from jax import lax
from jax.experimental import pallas as pl
from jax.experimental.pallas import tpu as pltpu
from jax.sharding import PartitionSpec as P

HIGH = lax.Precision.HIGHEST
MESH = pl.DeviceIdType.MESH
VMEM = pl.BlockSpec(memory_space=pltpu.VMEM)
ANY = pl.BlockSpec(memory_space=pl.ANY)
HBM = pl.BlockSpec(memory_space=pltpu.HBM)
BLK = 64
OUT = 4
WIDE = 512
ROOM = 44 << 20
SMALL = 2 << 20
GROUP = 8


def mm(x, y, cx, cy):
    return lax.dot_general(x, y, (((cx,), (cy,)), ((), ())), precision=HIGH, preferred_element_type=jnp.float32)


def split(x):
    top = x.astype(jnp.bfloat16)
    return top, (x - top.astype(jnp.float32)).astype(jnp.bfloat16)


def dot3(x, y, cx, cy):
    (xt, xl), (yt, yl) = x, y
    dot = functools.partial(lax.dot_general, dimension_numbers=(((cx,), (cy,)), ((), ())),
                            preferred_element_type=jnp.float32)
    return dot(xt, yt) + (dot(xt, yl) + dot(xl, yt))


def mm3(x, y, cx, cy):
    return dot3(split(x), split(y), cx, cy)


def remote(src, dst, send, recv, device):
    return pltpu.make_async_remote_copy(
        src_ref=src, dst_ref=dst, send_sem=send, recv_sem=recv, device_id=device, device_id_type=MESH)


def signal(device):
    pl.semaphore_signal(pltpu.get_barrier_semaphore(), inc=1, device_id=device, device_id_type=MESH)


def bits_of(n_row):
    bits = n_row.bit_length() - 1
    assert 1 << bits == n_row
    return bits


def row_partner(bit):
    row = lax.axis_index("row")
    return row + (1 << bit) - 2 * (1 << bit) * (lax.rem(row // (1 << bit), 2))


def row_parts(bits, acc, got, send, recv, base, size):
    half = size // 2

    def copy(step, part):
        bit = (step + part) % bits
        rows = pl.ds(base + part * half, half)
        at = base // size
        return remote(acc.at[step, rows], got.at[step, rows], send.at[at, step, part], recv.at[at, step, part],
                      {"row": row_partner(bit)})

    def begin():
        for part in range(2):
            copy(0, part).start()

    def meet(step):
        for part in range(2):
            rows = pl.ds(base + part * half, half)
            copy(step, part).wait_recv()
            acc[step + 1, rows, :] = acc[step, rows, :] + got[step, rows, :]
            if step + 1 < bits:
                copy(step + 1, part).start()

    def end():
        for step in range(bits):
            for part in range(2):
                copy(step, part).wait_send()

    return begin, meet, end


def factor_block(block):
    n = block.shape[0]
    eye = (lax.broadcasted_iota(jnp.int32, (n, n), 0) == lax.broadcasted_iota(jnp.int32, (n, n), 1)).astype(block.dtype)
    full = jnp.concatenate([block, eye], axis=1)
    groups = [full[8 * g:8 * g + 8, :] for g in range(n // 8)]
    sub = lax.broadcasted_iota(jnp.int32, (8, 2 * n), 0)
    for g in range(n // 8):
        cols = [[jnp.broadcast_to(groups[h][:, 8 * g + c:8 * g + c + 1], (8, 2 * n)) for c in range(8)]
                for h in range(g, n // 8)]
        heads = [[cols[0][c][r:r + 1, :] for c in range(8)] for r in range(8)]
        lines = [groups[g][r:r + 1, :] for r in range(8)]
        invs = []
        for p in range(8):
            inv = 1.0 / heads[p][p]
            invs.append(inv)
            for r in range(p + 1, 8):
                factor = heads[r][p] * inv
                lines[r] = lines[r] - factor * lines[p]
                for c in range(p + 1, 8):
                    heads[r][c] = heads[r][c] - factor * heads[p][c]
        for h in range(g + 1, n // 8):
            col = cols[h - g]
            total = groups[h]
            for p in range(8):
                factor = col[p] * invs[p]
                total = total - factor * lines[p]
                for c in range(p + 1, 8):
                    col[c] = col[c] - factor * heads[p][c]
            groups[h] = total
        group = jnp.broadcast_to(lines[0], (8, 2 * n))
        for r in range(1, 8):
            group = jnp.where(sub == r, lines[r], group)
        groups[g] = group
    full = jnp.concatenate(groups, axis=0)
    diag = jnp.sum(full[:, :n] * eye, axis=1, keepdims=True)
    return full[:, n:] * lax.rsqrt(diag)


def sweep_kernel(bits, chain, rank, scale, b_hbm, a_hbm, u_hbm, v_hbm, fu_hbm, fv_hbm, fleft_ref, fright_ref,
                 f, x, acc, got, own, cs, rs, ctop, clow, mtop, mlow, m, gpart, gmate, gacc, ggot, gfin, lp, lmate, lgot, lcross, lfull, lout,
                 tab, linv_ref, lout_ref, load, row_send, row_recv, own_send, own_recv, own_here, *more):
    c_sems, r_sems = more[:6], more[6:12]
    (gm_send, gm_recv, g_send, g_recv, gf_send, gf_recv, go_send, lm_send, lm_recv, lc_send, lc_recv, rs_send, rs_recv,
     ag_send, ag_recv, lh_send, lh_recv, lo_send, lo_recv, mo_send, m_recv, mp_send, mr_send, mf_send, store) = more[12:]
    tenant, row = lax.axis_index("tenant"), lax.axis_index("row")
    core, place = lax.rem(tenant, 2), tenant // 2
    nt, n_row = 2 * chain, 1 << bits
    low = chain // 2 - 1
    outs = chain // 2 - 1
    side = place // (chain // 2)
    is_mid = jnp.logical_or(place == low, place == low + 1)
    is_out = jnp.logical_not(is_mid)
    is_hub = jnp.logical_and(is_mid, core == 1)
    is_sub = jnp.logical_and(is_mid, core == 0)
    mate = {"tenant": tenant + 1 - 2 * core}
    across = {"tenant": 2 * (2 * low + 1 - place) + core}
    nb = bits + 1
    rows, width = f.shape[1:]
    k = x.shape[2]
    kh = k // 2
    wq = width // 4
    half = nt * rows // 2
    piece = half // n_row
    mine = 2 * side + core
    wide = min(WIDE, wq)

    def outer(j):
        return (1 - side) * (low - 1 - j) + side * (low + 2 + j)

    def out_device(j):
        return {"tenant": 2 * outer(j) + core}

    def neighbour(d):
        to = row
        for bit in range(bits):
            if d >> bit & 1:
                to = to + (1 << bit) - 2 * (1 << bit) * lax.rem(to // (1 << bit), 2)
        return to

    pairs = ((b_hbm, f.at[0]), (u_hbm, x.at[0]), (a_hbm, f.at[1]), (v_hbm, x.at[1]))
    loads = [pltpu.make_async_copy(src, dst, load.at[i]) for i, (src, dst) in enumerate(pairs)]
    for copy in loads:
        copy.start()
    for d in range(1, nt):
        signal({"tenant": lax.rem(tenant + d, nt)})
    for d in range(1, n_row):
        signal({"row": lax.rem(row + d, n_row)})

    @pl.when(is_mid)
    def _():
        for d in range(1, n_row):
            signal({"tenant": 2 * (2 * low + 1 - place) + core, "row": lax.rem(row + d, n_row)})

    def ship(fac, q, lines=None):
        cols = pl.ds(q * wq, wq)
        target = 2 * (low + q // 2) + q % 2
        lines = lines or pl.ds(0, rows)
        sent = remote(f.at[fac, lines, cols], own.at[fac, tenant, lines], own_send.at[fac, q], own_recv.at[fac, tenant],
                      {"tenant": target})
        kept = pltpu.make_async_copy(f.at[fac, :, cols], own.at[fac, tenant], own_here.at[fac])
        return target, sent, kept

    def near(target):
        return target // 2 // (chain // 2) == side

    def far(target):
        return target // 2 // (chain // 2) != side

    def ship_all(fac, some, cores=(0, 1), lines=None):
        for q in [2 * h + c for h in range(2) for c in cores]:
            target, sent, kept = ship(fac, q, lines)

            @pl.when(jnp.logical_and(tenant != target, some(target)))
            def _(sent=sent):
                sent.start()

            if some is not far:
                @pl.when(tenant == target)
                def _(kept=kept):
                    kept.start()

    def ship_end(fac):
        for q in range(4):
            target, sent, kept = ship(fac, q)

            @pl.when(tenant != target)
            def _(sent=sent):
                sent.wait_send()

    def own_wait(fac):
        cols = pl.ds(pl.multiple_of(mine * wq, wq), wq)
        pltpu.make_async_copy(f.at[fac, :, cols], own.at[fac, tenant], own_here.at[fac]).wait()

        def one(i, _):
            @pl.when(i != tenant)
            def _():
                remote(own.at[fac, i], own.at[fac, i], own_send.at[fac, 0], own_recv.at[fac, i], mate).wait_recv()

            return 0

        lax.fori_loop(0, nt, one, 0)

    top, bottom = pl.ds(0, rows // 2), pl.ds(rows // 2, rows - rows // 2)
    tile = 512 if width % 512 == 0 else width
    acc[0] = jnp.zeros_like(acc[0])
    parts = [row_parts(bits, acc, got, row_send, row_recv, fac * rows, rows) for fac in range(2)]
    for fac in range(2):
        loads[2 * fac].wait()
        if fac == 0:
            pl.semaphore_wait(pltpu.get_barrier_semaphore(), nt - 1 + (n_row - 1) * (1 + is_mid.astype(jnp.int32)))

            ship_all(0, near)

            @pl.when(is_mid)
            def _():
                ship_all(0, far)

            @pl.when(is_out)
            def _():
                ship_all(0, far, (1,), top)

        loads[2 * fac + 1].wait()

        def step(i, _, fac=fac):
            cols = pl.ds(pl.multiple_of(i * tile, tile), tile)
            acc[0, pl.ds(fac * rows, rows), :] += mm3(f[fac, :, cols], x[fac, cols, :], 1, 0)
            return 0

        lax.fori_loop(0, width // tile, step, 0)
        parts[fac][0]()
    for at in range(bits):
        for fac in range(2):
            parts[fac][1](at)

    same = lax.broadcasted_iota(jnp.int32, (rows, rows), 0) // rank == lax.broadcasted_iota(
        jnp.int32, (rows, rows), 1) // rank
    rq = rows // n_row
    strip = pl.ds(pl.multiple_of(row * rq, 8), rq)
    below = acc[bits, pl.ds(pl.multiple_of(rows + row * rq, 8), rq), :]
    own_rank = (row * rq + lax.broadcasted_iota(jnp.int32, (rq, rows), 0)) // rank == lax.broadcasted_iota(
        jnp.int32, (rq, rows), 1) // rank
    weight = jnp.where(own_rank, mm(below, acc[bits, rows:, :], 1, 1), 0.0)
    cs[0, place, core, strip, :] = mm(weight, acc[bits, :rows, :], 1, 0)
    rs[place, core, strip, :] = below

    def hand(buf, sems, hop):
        to = low + hop
        part = buf.at[place, core, strip]
        return to, remote(part, part, sems[0].at[hop], sems[1].at[place], {"tenant": 2 * to + core})

    def hand_all(buf, sems):
        for hop in range(2):
            to, sent = hand(buf, sems, hop)

            @pl.when(place != to)
            def _(sent=sent):
                sent.start()

    def spread_copy(buf, sems, d):
        to = neighbour(d)
        part = buf.at[:, core, strip]
        return to, remote(part, part, sems[2].at[d - 1], sems[3].at[row], {"row": to})

    def spread_mate(buf, sems):
        part = buf.at[:, core]
        return remote(part, part, sems[4].at[0], sems[5].at[0], mate)

    def spread_begin(buf, sems):
        def take(i, _):
            @pl.when(i != place)
            def _():
                part = buf.at[i, core, strip]
                remote(part, part, sems[0].at[0], sems[1].at[i], mate).wait_recv()

            return 0

        lax.fori_loop(0, chain, take, 0)
        for d in range(1, n_row):
            spread_copy(buf, sems, d)[1].start()

    def spread_meet(buf, sems):
        for d in range(1, n_row):
            to = spread_copy(buf, sems, d)[0]
            part = buf.at[:, core, pl.ds(pl.multiple_of(to * rq, 8), rq)]
            remote(part, part, sems[2].at[0], sems[3].at[to], mate).wait_recv()
        spread_mate(buf, sems).start()

    def spread_rest(buf, sems):
        part = buf.at[:, 1 - core]
        remote(part, part, sems[4].at[0], sems[5].at[0], mate).wait_recv()

    def spread_end(buf, sems):
        for hop in range(2):
            to, sent = hand(buf, sems, hop)

            @pl.when(place != to)
            def _(sent=sent):
                sent.wait_send()

        @pl.when(is_mid)
        def _():
            for d in range(1, n_row):
                spread_copy(buf, sems, d)[1].wait_send()
            spread_mate(buf, sems).wait_send()

    first = cs.at[0]
    hand_all(first, c_sems)

    hand_all(rs, r_sems)

    @pl.when(is_out)
    def _():
        ship_all(0, far, (1,), bottom)
        ship_all(0, far, (0,))
        ship_all(1, far)

    ship_all(1, near)

    for fac in range(2):
        parts[fac][2]()

    def quarter_out(ph, j):
        return remote(m.at[ph, mine], m.at[ph, mine], mo_send.at[ph, j], m_recv.at[ph, mine], out_device(j))

    def quarter_across(ph, c):
        part = m.at[ph, 2 * side + c]
        return remote(part, part, mp_send.at[ph, c], m_recv.at[ph, 2 * side + c], across)

    def quarter_relay(ph, c, j):
        at = 2 * (1 - side) + c
        return remote(m.at[ph, at], m.at[ph, at], mr_send.at[ph, c, j], m_recv.at[ph, at], out_device(j))

    def quarter_mate(ph, at):
        return remote(m.at[ph, at], m.at[ph, at], mf_send.at[ph, at], m_recv.at[ph, at], mate)

    def quarter_wait(ph, at):
        remote(m.at[ph, at], m.at[ph, at], mp_send.at[ph, 0], m_recv.at[ph, at], mate).wait_recv()

    def cross(ph):
        quarter_across(ph, 0).start()
        quarter_wait(ph, 2 * side + 1)
        quarter_across(ph, 1).start()

    distant = [2 * (1 - side) + c for c in range(2)]

    def relay(ph, c):
        quarter_wait(ph, distant[c])
        quarter_mate(ph, distant[c]).start()
        if c == 0:
            for j in range(outs):
                quarter_relay(ph, c, j).start()

    def relay_hub(ph):
        quarter_wait(ph, distant[1])
        for j in range(outs):
            quarter_relay(ph, 1, j).start()

    def gram_mate(ph):
        return remote(gpart.at[ph], gmate.at[ph], gm_send.at[ph], gm_recv.at[ph], mate)

    def gram_copy(ph, at, part):
        dim = (at + part) % nb
        device = across if dim == bits else {"row": row_partner(dim)}
        return remote(gacc.at[ph, at, part], ggot.at[ph, at, part], g_send.at[ph, at, part], g_recv.at[ph, at, part], device)

    def gram_down(ph):
        return remote(gfin.at[ph], gfin.at[ph], gf_send.at[ph], gf_recv.at[ph], mate)

    def gram_out(ph, j):
        return remote(gfin.at[ph], gfin.at[ph], go_send.at[ph, j], gf_recv.at[ph], out_device(j))

    def gram_meet(ph, at):
        for part in range(3):
            gram_copy(ph, at, part).wait_recv()
            total = gacc[ph, at, part] + ggot[ph, at, part]
            if at + 1 < nb:
                gacc[ph, at + 1, part] = total
                gram_copy(ph, at + 1, part).start()
            else:
                gfin[ph, part] = total

    def left_mate(ph):
        there = pl.ds(pl.multiple_of((1 - core) * half, half), half)
        return remote(lp.at[ph, there], lmate.at[ph], lm_send.at[ph], lm_recv.at[ph], mate)

    def piece_at(at):
        return pl.ds(pl.multiple_of(core * half + at * piece, 8), piece)

    def left_copy(ph, d):
        to = neighbour(d)
        return remote(lp.at[ph, piece_at(to)], lgot.at[ph, row], rs_send.at[ph, d - 1], rs_recv.at[ph, row], {"row": to})

    def left_cross(ph):
        return remote(lp.at[ph, piece_at(row)], lcross.at[ph], lc_send.at[ph], lc_recv.at[ph], across)

    def left_share(ph, d):
        part = lfull.at[ph, piece_at(row)]
        return remote(part, part, ag_send.at[ph, d - 1], ag_recv.at[ph, row], {"row": neighbour(d)})

    def left_half(ph):
        here = pl.ds(pl.multiple_of(core * half, half), half)
        return remote(lfull.at[ph, here], lfull.at[ph, here], lh_send.at[ph], lh_recv.at[ph], mate)

    def left_out(ph, j, c):
        to = 2 * outer(j) + c
        here = pl.ds(pl.multiple_of(to * rows, rows), rows)
        return remote(lfull.at[ph, here], lout.at[ph], lo_send.at[ph, j, c], lo_recv.at[ph], {"tenant": to})

    def left_sum(ph):
        for d in range(1, n_row):
            to = neighbour(d)
            remote(lgot.at[ph, to], lgot.at[ph, to], rs_send.at[ph, 0], rs_recv.at[ph, to], mate).wait_recv()
        total = lp[ph, piece_at(row), :]
        for at in range(n_row):
            total += lgot[ph, at]
        lp[ph, piece_at(row), :] = total
        left_cross(ph).start()

    def left_join(ph):
        left_cross(ph).wait_recv()
        lfull[ph, piece_at(row), :] = lp[ph, piece_at(row), :] + lcross[ph]
        for d in range(1, n_row):
            left_share(ph, d).start()

    lgot[0, row] = jnp.zeros_like(lgot[0, 0])
    lgot[1, row] = jnp.zeros_like(lgot[1, 0])

    def body(ph, _):
        @pl.when(is_mid)
        def _():
            @pl.when(ph == 0)
            def _():
                spread_begin(first, c_sems)
                spread_meet(first, c_sems)
                spread_rest(first, c_sems)

            own_wait(ph)
            coeffs = cs[ph].reshape(nt * rows, k)
            ctop[...], clow[...] = split(coeffs)

            def columns(j, _):
                cols = pl.ds(pl.multiple_of(j * wide, wide), wide)
                here = pl.ds(pl.multiple_of(j * wide, wide), wide)
                block = own[ph, :, :, cols].reshape(nt * rows, wide)
                total = dot3(split(block), (ctop[...], clow[...]), 0, 0)
                m[ph, mine, here, :] = total
                mtop[here, :], mlow[here, :] = split(total)
                return 0

            lax.fori_loop(0, wq // wide, columns, 0)
            for j in range(outs):
                quarter_out(ph, j).start()
            quarter_mate(ph, mine).start()
            mq = m.at[ph, mine]
            upper = mm(mq[:, :kh], mq[...], 0, 0)
            grams = (upper[:, :kh], upper[:, kh:], mm(mq[:, kh:], mq[:, kh:], 0, 0))
            for part in range(3):
                gpart[ph, part] = grams[part]

            @pl.when(core == 0)
            def _():
                gram_mate(ph).start()

            @pl.when(core == 1)
            def _():
                gram_mate(ph).wait_recv()
                for part in range(3):
                    gacc[ph, 0, part] = gpart[ph, part] + gmate[ph, part]
                    gram_copy(ph, 0, part).start()

            def lefts(i, _):
                here = pl.ds(pl.multiple_of(i * rows, rows), rows)
                lp[ph, here, :] = dot3(split(own[ph, i]), (mtop[...], mlow[...]), 1, 0)
                return 0

            lax.fori_loop(0, nt, lefts, 0)
            left_mate(ph).start()

            order = sorted(range(1, n_row), key=lambda d: (bin(d).count("1"), d))
            share = -(-len(order) // nb)

            def lefts_ready():
                left_mate(ph).wait_recv()
                here = pl.ds(pl.multiple_of(core * half, half), half)
                lp[ph, here, :] += lmate[ph]

            @pl.when(core == 1)
            def _():
                @pl.when(ph == 0)
                def _():
                    lefts_ready()
                    for d in order:
                        left_copy(0, d).start()

                gram_meet(ph, 0)

                @pl.when(ph == 1)
                def _():
                    lefts_ready()

                for at in range(nb):
                    if at == nb - 1:
                        @pl.when(ph == 0)
                        def _():
                            left_sum(0)
                            spread_begin(rs, r_sems)

                    if at:
                        gram_meet(ph, at)
                    if at == nb - 1:
                        gram_down(ph).start()
                        for j in range(outs):
                            gram_out(ph, j).start()

                    @pl.when(ph == 1)
                    def _(at=at):
                        for d in order[at * share:(at + 1) * share]:
                            left_copy(1, d).start()

                @pl.when(ph == 1)
                def _():
                    relay_hub(0)
                    left_sum(1)

            @pl.when(core == 0)
            def _():
                @pl.when(ph == 1)
                def _():
                    cross(1)

                lefts_ready()
                for d in order:
                    left_copy(ph, d).start()

                @pl.when(ph == 1)
                def _():
                    relay(0, 0)
                    relay(0, 1)
                    left_sum(1)
                    relay(1, 0)

                @pl.when(ph == 0)
                def _():
                    spread_begin(rs, r_sems)
                    left_sum(0)
                    ship_all(1, far)

                gram_down(ph).wait_recv()

            @pl.when(jnp.logical_and(ph == 0, core == 1))
            def _():
                left_join(0)
                ship_all(1, far)

        @pl.when(is_out)
        def _():
            gram_down(ph).wait_recv()

            @pl.when(core == 1)
            def _():
                gram_down(ph).start()

        tab[:kh, :kh] = gfin[ph, 0]
        tab[:kh, kh:k] = gfin[ph, 1]
        tab[kh:, kh:k] = gfin[ph, 2]
        tab[:, k:] = (lax.broadcasted_iota(jnp.int32, (k, k), 0) == lax.broadcasted_iota(
            jnp.int32, (k, k), 1)).astype(jnp.float32)
        for at in range(0, k, BLK):
            end = at + BLK
            small = factor_block(tab[at:end, at:end])
            done = mm(small, tab[at:end, at:], 1, 0)
            tab[at:end, at:] = done
            if end < k:
                tab[end:, end:] -= mm(done[:, end - at:k - at], done[:, end - at:], 0, 0)
            if at == BLK:
                @pl.when(jnp.logical_and(is_hub, ph == 1))
                def _():
                    relay_hub(1)
            if at == 0:
                @pl.when(jnp.logical_and(is_sub, ph == 0))
                def _():
                    left_join(0)

                @pl.when(jnp.logical_and(is_mid, ph == 1))
                def _():
                    left_join(1)

                    @pl.when(core == 0)
                    def _():
                        relay(1, 1)

            if at == 2 * BLK:
                @pl.when(is_mid)
                def _():
                    @pl.when(jnp.logical_and(ph == 0, core == 0))
                    def _():
                        cross(0)
        linv_ref[ph] = tab[:, k:]

        @pl.when(is_mid)
        def _():
            for d in range(1, n_row):
                part = lfull.at[ph, piece_at(neighbour(d))]
                remote(part, part, ag_send.at[ph, 0], ag_recv.at[ph, neighbour(d)], mate).wait_recv()
            left_half(ph).start()

            @pl.when(ph == 0)
            def _():
                spread_meet(rs, r_sems)

            left_half(ph).wait_recv()

            @pl.when(ph == 0)
            def _():
                spread_rest(rs, r_sems)

            @pl.when(core == 1)
            def _():
                for j in range(outs):
                    for c in range(2):
                        left_out(ph, j, c).start()

            lout_ref[ph] = lfull[ph, pl.ds(pl.multiple_of(tenant * rows, rows), rows), :]

            @pl.when(ph == 0)
            def _():
                inverse = split(tab[:, k:])

                def some(i, _):
                    group = range(GROUP)
                    ats = [i * GROUP + j for j in group]
                    lefts = [split(dot3(split(lfull[0, pl.ds(pl.multiple_of(at * rows, rows), rows), :]), inverse, 1, 1))
                             for at in ats]
                    weights = [split(jnp.where(same, dot3(left, left, 1, 1), 0.0)) for left in lefts]
                    for j in group:
                        at = ats[j]
                        cs[1, at // 2, at % 2] = dot3(weights[j], split(rs[at // 2, at % 2]), 1, 0)
                    return 0

                lax.fori_loop(0, nt // GROUP, some, 0)

        return 0

    lax.fori_loop(0, 2, body, 0)

    def keep(ph, at):
        here = pl.ds(pl.multiple_of(at * wq, wq), wq)
        return pltpu.make_async_copy(x.at[ph, here], (fu_hbm, fv_hbm)[ph].at[here], store.at[ph, at])

    def quarter_done(ph, at, inverse):
        here = pl.ds(pl.multiple_of(at * wq, wq), wq)
        x[ph, here, :] = dot3(split(m[ph, at]), inverse, 1, 1)

    near_mine, near_mate = mine, 2 * side + 1 - core

    def fetch_near(ph):
        @pl.when(is_out)
        def _():
            quarter_wait(ph, near_mine)
            quarter_mate(ph, near_mine).start()

    def fetch_far(ph):
        @pl.when(is_out)
        def _():
            at = 2 * (1 - side) + core
            quarter_wait(ph, at)
            quarter_mate(ph, at).start()

    def fetch_rest(ph):
        @pl.when(is_out)
        def _():
            quarter_wait(ph, 2 * (1 - side) + 1 - core)

        @pl.when(is_hub)
        def _():
            quarter_wait(ph, distant[0])

    def fetch_mate(ph):
        @pl.when(jnp.logical_or(core == 1, is_out))
        def _():
            quarter_wait(ph, near_mate)

    def fetch_part(ph):
        @pl.when(is_out)
        def _():
            remote(lout.at[ph], lout.at[ph], lo_send.at[ph, 0, 0], lo_recv.at[ph], mate).wait_recv()
            lout_ref[ph] = lout[ph]

        (fleft_ref, fright_ref)[ph][...] = mm3(lout_ref[ph], linv_ref[ph], 1, 1)

    def give(ph, at):
        quarter_done(ph, at, inverses[ph])
        keep(ph, at).start()

    inverses = [split(linv_ref[ph] * scale) for ph in range(2)]
    for ph in range(2):
        fetch_near(ph)
    fetch_far(0)
    give(0, near_mine)
    give(1, near_mine)
    for ph in range(2):
        fetch_mate(ph)
    fetch_rest(0)
    for at in [near_mate] + distant:
        give(0, at)
    give(1, near_mate)
    fetch_far(1)
    give(1, 2 * (1 - side) + core)
    fetch_part(0)
    fetch_rest(1)
    give(1, 2 * (1 - side) + 1 - core)
    fetch_part(1)
    ship_end(0)
    ship_end(1)
    spread_end(first, c_sems)
    spread_end(rs, r_sems)

    def drain(ph, _):
        quarter_mate(ph, mine).wait_send()

        @pl.when(is_out)
        def _():
            quarter_mate(ph, 2 * (1 - side) + core).wait_send()

        @pl.when(is_mid)
        def _():
            for j in range(outs):
                quarter_out(ph, j).wait_send()
            left_mate(ph).wait_send()
            left_half(ph).wait_send()
            for d in range(1, n_row):
                left_copy(ph, d).wait_send()
                left_share(ph, d).wait_send()
            left_cross(ph).wait_send()

        @pl.when(is_sub)
        def _():
            gram_mate(ph).wait_send()
            for c in range(2):
                quarter_across(ph, c).wait_send()
                quarter_mate(ph, distant[c]).wait_send()
            for j in range(outs):
                quarter_relay(ph, 0, j).wait_send()

        @pl.when(core == 1)
        def _():
            gram_down(ph).wait_send()

        @pl.when(is_hub)
        def _():
            for j in range(outs):
                gram_out(ph, j).wait_send()
                quarter_relay(ph, 1, j).wait_send()
                for c in range(2):
                    left_out(ph, j, c).wait_send()
            for at in range(nb):
                for part in range(3):
                    gram_copy(ph, at, part).wait_send()

        return 0

    lax.fori_loop(0, 2, drain, 0)
    for ph in range(2):
        for at in range(4):
            keep(ph, at).wait()


def sweep(bits, chain, rank, scale, b, a, u, v):
    rows, width = b.shape
    k = u.shape[1]
    kh, wq = k // 2, width // 4
    nt, n_row = 2 * chain, 1 << bits
    outs, nb = max(chain // 2 - 1, 1), bits + 1
    half = nt * rows // 2
    f32, b16 = jnp.float32, jnp.bfloat16
    dma = pltpu.SemaphoreType.DMA
    big, small = jax.ShapeDtypeStruct((width, k), f32), jax.ShapeDtypeStruct((rows, k), f32)
    return pl.pallas_call(
        functools.partial(sweep_kernel, bits, chain, rank, scale),
        out_shape=(big, big, small, small),
        in_specs=[HBM] * 4,
        out_specs=(ANY, ANY, VMEM, VMEM),
        scratch_shapes=[
            pltpu.VMEM((2, rows, width), f32),
            pltpu.VMEM((2, width, k), f32),
            pltpu.VMEM((bits + 1, 2 * rows, k), f32),
            pltpu.VMEM((bits, 2 * rows, k), f32),
            pltpu.VMEM((2, nt, rows, wq), f32),
            pltpu.VMEM((2, chain, 2, rows, k), f32),
            pltpu.VMEM((chain, 2, rows, k), f32),
            pltpu.VMEM((nt * rows, k), b16),
            pltpu.VMEM((nt * rows, k), b16),
            pltpu.VMEM((wq, k), b16),
            pltpu.VMEM((wq, k), b16),
            pltpu.VMEM((2, 4, wq, k), f32),
            pltpu.VMEM((2, 3, kh, kh), f32),
            pltpu.VMEM((2, 3, kh, kh), f32),
            pltpu.VMEM((2, nb, 3, kh, kh), f32),
            pltpu.VMEM((2, nb, 3, kh, kh), f32),
            pltpu.VMEM((2, 3, kh, kh), f32),
            pltpu.VMEM((2, nt * rows, k), f32),
            pltpu.VMEM((2, half, k), f32),
            pltpu.VMEM((2, n_row, half // n_row, k), f32),
            pltpu.VMEM((2, half // n_row, k), f32),
            pltpu.VMEM((2, nt * rows, k), f32),
            pltpu.VMEM((2, rows, k), f32),
            pltpu.VMEM((k, 2 * k), f32),
            pltpu.VMEM((2, k, k), f32),
            pltpu.VMEM((2, rows, k), f32),
            dma((4,)), dma((2, bits, 2)), dma((2, bits, 2)),
            dma((2, 4)), dma((2, nt)), dma((2,)),
            dma((2,)), dma((chain,)), dma((n_row,)), dma((n_row,)), dma((1,)), dma((1,)),
            dma((2,)), dma((chain,)), dma((n_row,)), dma((n_row,)), dma((1,)), dma((1,)),
            dma((2,)), dma((2,)), dma((2, nb, 3)), dma((2, nb, 3)), dma((2,)), dma((2,)), dma((2, outs)),
            dma((2,)), dma((2,)), dma((2,)), dma((2,)), dma((2, n_row)), dma((2, n_row)), dma((2, n_row)), dma((2, n_row)),
            dma((2,)), dma((2,)), dma((2, outs, 2)), dma((2,)),
            dma((2, outs)), dma((2, 4)), dma((2, 2)), dma((2, 2, outs)), dma((2, 4)), dma((2, 4)),
        ],
        compiler_params=pltpu.CompilerParams(collective_id=0, has_side_effects=True, vmem_limit_bytes=ROOM),
    )(b, a, u, v)


def finish_kernel(u_any, v_any, left_in, right_in, fu_hbm, fv_hbm, left_ref, right_ref, store):
    ins, outs = (u_any, v_any), (fu_hbm, fv_hbm)
    size = u_any.shape[0] // OUT
    spots = [(s, i, pl.ds(i * size, size)) for s in range(2) for i in range(OUT)]
    stores = [pltpu.make_async_copy(ins[s].at[at], outs[s].at[at], store.at[s, i]) for s, i, at in spots]
    for copy in stores:
        copy.start()
    left_ref[...] = left_in[...]
    right_ref[...] = right_in[...]
    for copy in stores:
        copy.wait()


def finish(u, v, left, right):
    big, small = jax.ShapeDtypeStruct(u.shape, u.dtype), jax.ShapeDtypeStruct(left.shape, left.dtype)
    return pl.pallas_call(
        finish_kernel,
        out_shape=(big, big, small, small),
        in_specs=[ANY, ANY, VMEM, VMEM],
        out_specs=(HBM, HBM, VMEM, VMEM),
        scratch_shapes=[pltpu.SemaphoreType.DMA((2, OUT))],
        compiler_params=pltpu.CompilerParams(vmem_limit_bytes=SMALL),
    )(u, v, left, right)


def local(mesh_shape, b_factors, a_factors, u_start, v_start):
    nt, rank, width = b_factors.shape
    rows = nt * rank
    k = u_start.shape[1]
    bits = bits_of(mesh_shape["row"])
    chain = mesh_shape["tenant"] // 2
    scale = math.sqrt(width * mesh_shape["row"])
    arrays = (b_factors.reshape(rows, width), a_factors.reshape(rows, width), u_start, v_start)
    swept = sweep(bits, chain, rank, scale, *(pltpu.with_memory_space_constraint(x, pltpu.HBM) for x in arrays))
    u, v, left, right = finish(*swept)
    return u, v, left.reshape(nt, rank, k), right.reshape(nt, rank, k)


def solution(mesh):
    in_specs = (P("tenant", None, "row"), P("tenant", None, "row"), P("row", None), P("row", None))
    out_specs = (P("row", None), P("row", None), P("tenant", None, None), P("tenant", None, None))
    return jax.shard_map(functools.partial(local, dict(mesh.shape)), mesh=mesh, in_specs=in_specs,
                         out_specs=out_specs, check_vma=False)
```
